128 devices in a mesh: row: 8 (over x, y_lo), col: 16 (over z, y_hi, core).
Axes of the slice: x: 4, y: 4 (y_hi: 2, y_lo: 2; y = y_hi * 2 + y_lo), z: 4, core: 2. Of those that a mesh axis runs over, the one named last changes fastest.
Arguments:
- elevation: float32 [4096, 16384], P('row', 'col'), may hold values from -6 to 6
- ocean: int32 [4096, 16384], P('row', 'col'), may hold values from 0 to 1, as said below
- outlet: int32 [4096, 16384], P('row', 'col'), may hold values from 0 to 1, as said below
Outputs:
- surface: float32 [4096, 16384], P('row', 'col')
The draws below stay inside these ranges and needn't reach their ends.
Inputs may be any that keep to these rules, and one draw needn't show every extreme that they name: ocean cells are scattered; no bound on their count in any region may be assumed. outlet cells are scattered; no bound on their count in any region may be assumed.
All inputs are finite; a program needn't handle non-finite values.
Results may differ from the reference program's by a relative error of at most 0.00002.
Values sent between devices are 32-bit elements; how exact they have to be, the bound alone decides.
A program may use at most 128 MiB of HBM per device.

```python
import jax
import jax.numpy as jnp
from jax import lax

BLK = 16
COARSE = 4
FINE = 8
NX = 4096
NY = 16384


def dry_patch(key):
    anchor_key = jax.random.fold_in(key, 7)
    row_key, col_key = jax.random.split(anchor_key)
    block_rows = NX // BLK
    block_cols = NY // BLK
    top_row = jax.random.randint(row_key, (), 0, block_rows - 9) * BLK
    left_col = jax.random.randint(col_key, (), 0, block_cols - 9) * BLK
    rows_iota = lax.broadcasted_iota(jnp.int32, (NX, NY), 0)
    cols_iota = lax.broadcasted_iota(jnp.int32, (NX, NY), 1)
    inside_rows = (rows_iota >= top_row) & (rows_iota < top_row + 10 * BLK)
    inside_cols = (cols_iota >= left_col) & (cols_iota < left_col + 10 * BLK)
    return inside_rows & inside_cols


def draw_ocean(key, part):
    hits = jax.random.randint(jax.random.fold_in(key, 11), (NX, NY), 0, 512)
    marked = (hits == 0) & jnp.logical_not(dry_patch(key))
    return jnp.where(marked, 1, 0).astype(jnp.int32)


def draw_outlet(key, part):
    hits = jax.random.randint(jax.random.fold_in(key, 13), (NX, NY), 0, 1024)
    marked = (hits == 0) & jnp.logical_not(dry_patch(key))
    return jnp.where(marked, 1, 0).astype(jnp.int32)


def shard_levels(key, dims, shards, least, high):
    factor_of = 1.0
    for axis_at, blocks in shards:
        draws = jax.random.uniform(jax.random.fold_in(jax.random.fold_in(key, 6), axis_at), (blocks,), jnp.float32, least / len(shards), high / len(shards))
        factor_of = factor_of * jnp.repeat(jnp.exp(draws), dims[axis_at] // blocks).reshape((-1,) + (1,) * (len(dims) - 1 - axis_at))
    return factor_of


def centred(rng, shape, scale, reach, shards=(), kind=jnp.bfloat16):
    values = jax.random.normal(rng, shape, jnp.float32) * scale
    if len(shards) > 0:
        values = shard_levels(rng, shape, shards, -0.22, 0.18) * values
    return jnp.clip(values, min=-reach, max=reach).astype(kind)


def setup_inputs(seed: int = 0) -> dict:
    streams_of = jax.random.split(jax.random.key(seed), 4)
    elevation = centred(streams_of[0], (NX, NY), 1.0, 6.0, ((0, 8), (1, 16)), jnp.float32)
    ocean = draw_ocean(jax.random.fold_in(streams_of[3], 71), 0)
    outlet = draw_outlet(jax.random.fold_in(streams_of[3], 71), 0)
    return {"elevation": elevation, "ocean": ocean, "outlet": outlet}


huge_level = 1.0e30
fine_step = 2.0 ** -10
coarse_step = 2.0 ** -6


def extend(field):
    wrapped = jnp.concatenate([field[:, -1:], field, field[:, :1]], axis=1)
    return jnp.pad(wrapped, ((1, 1), (0, 0)), constant_values=huge_level)


def neighbour_min(extended):
    height = extended.shape[0] - 2
    width = extended.shape[1] - 2
    result = None
    for down in range(3):
        for across in range(3):
            if down == 1 and across == 1:
                continue
            piece = extended[down:down + height, across:across + width]
            result = piece if result is None else jnp.minimum(result, piece)
    return result


def update(extended, ground, lock, step_size):
    center = extended[1:-1, 1:-1]
    lowered = jnp.minimum(center, neighbour_min(extended) + step_size)
    return jnp.minimum(jnp.maximum(ground, lowered), lock)


def reference(elevation, ocean, outlet):
    ground = jnp.where(ocean == 1, jnp.float32(0.0), elevation)
    drains = (ocean == 1) | (outlet == 1)
    lock = jnp.where(drains, ground, jnp.float32(huge_level))
    shape_blocks = (NX // BLK, BLK, NY // BLK, BLK)
    ground_c = ground.reshape(shape_blocks).min(axis=(1, 3))
    lock_c = lock.reshape(shape_blocks).min(axis=(1, 3))
    coarse = ground.reshape(shape_blocks).max(axis=(1, 3))
    for sweep in range(COARSE):
        coarse = update(extend(coarse), ground_c, lock_c, coarse_step)
    lifted = jnp.repeat(jnp.repeat(coarse, BLK, axis=0), BLK, axis=1)
    surface = jnp.minimum(jnp.maximum(ground, lifted), lock)
    for sweep in range(FINE):
        surface = update(extend(surface), ground, lock, fine_step)
    return surface
```

```python
import jax
import jax.numpy as jnp
from jax import lax
from jax.experimental import pallas as pl
from jax.experimental.pallas import tpu as pltpu
from jax.sharding import PartitionSpec as P

MESH = pl.DeviceIdType.MESH
HUGE = 1e30
FINE_STEP = 2.0 ** (-10)
COARSE_STEP = 2.0 ** (-6)
F32 = jnp.float32

K = 33
W = 144
A = 18

DIRS = [(-1, 0), (1, 0), (0, -1), (0, 1), (-1, -1), (-1, 1), (1, -1), (1, 1)]
N_, S_, W_, E_, NW_, NE_, SW_, SE_ = range(8)
OPP = [S_, N_, E_, W_, SE_, SW_, NE_, NW_]


def lanes():
    return lax.broadcasted_iota(jnp.int32, (8, 128), 1)


def subs():
    return lax.broadcasted_iota(jnp.int32, (8, 128), 0)


def merge(a, b, w, axis, pos, op):
    size = 8 if axis == 0 else 128
    low = (pos & w) == 0
    p = jnp.where(low, a, b)
    q = jnp.where(low, pltpu.roll(a, size - w, axis), pltpu.roll(b, w, axis))
    return op(p, q)


def tree(xs, ws, axis, pos, op):
    for w in ws:
        half = len(xs) // 2
        xs = [merge(xs[i], xs[i + half], w, axis, pos, op) for i in range(half)]
    return xs[0]


def neighbour(d, rows, cols):
    r = lax.axis_index("row")
    c = lax.axis_index("col")
    return (lax.rem(r + d[0] + rows, rows), lax.rem(c + d[1] + cols, cols))


def sweep(src, dst, g):
    def row(ref, k):
        return [ref[k, pl.ds(a, 8, stride=A), :] for a in range(A)]

    def across(vm):
        before = pltpu.roll(vm[A - 1], 1, 0)
        after = pltpu.roll(vm[0], 7, 0)
        m = [None] * A
        for a in range(0, A, 2):
            q = jnp.minimum(vm[a], vm[a + 1])
            m[a] = jnp.minimum(vm[a - 1] if a else before, q)
            m[a + 1] = jnp.minimum(q, vm[a + 2] if a + 2 < A else after)
        return m

    def put(k, v, m):
        out = []
        for a in range(A):
            x = jnp.maximum(g[k, pl.ds(a, 8, stride=A), :], jnp.minimum(v[a], m[a] + FINE_STEP))
            dst[k + 1, pl.ds(a, 8, stride=A), :] = x
            out.append(x)
        return out

    def pair(k):
        v0, v1, v2, v3 = (row(src, k + i) for i in range(4))
        p = [jnp.minimum(x, y) for x, y in zip(v1, v2)]
        m0 = across([jnp.minimum(x, y) for x, y in zip(v0, p)])
        m1 = across([jnp.minimum(x, y) for x, y in zip(p, v3)])
        return put(k, v1, m0), put(k + 1, v2, m1)

    v0, v1, v2 = (row(src, K - 1 + i) for i in range(3))
    last = put(K - 1, v1, across([jnp.minimum(jnp.minimum(x, y), z) for x, y, z in zip(v0, v1, v2)]))
    for a in range(A):
        dst[0, pl.ds(a, 8, stride=A), :] = pltpu.roll(last[a], 1, 1)
    first, _ = pair(0)
    for a in range(A):
        dst[K + 1, pl.ds(a, 8, stride=A), :] = pltpu.roll(first[a], 127, 1)

    def body(i, c):
        pair(2 + 2 * i)
        return c

    lax.fori_loop(0, (K - 3) // 2, body, 0)


def kernel(rows, cols, e_h, oc_h, ou_h, o_h, ev, ocv, ouv, gl, halo, tt, va, vb, ov, ca, cp, pk, cn, pwe, cf, zz,
           yy, xb, fs, fr, cs, cr, ht, in_sem, out_sem, send, recv):
    lane = lanes()
    sub = subs()
    north = lax.axis_index("row") == 0
    south = lax.axis_index("row") == rows - 1
    to = [neighbour(d, rows, cols) for d in DIRS]

    barrier = pltpu.get_barrier_semaphore()
    for dev in to:
        pl.semaphore_signal(barrier, inc=1, device_id=dev, device_id_type=MESH)

    def loads(j):
        at = pl.ds(128 * j, 128)
        return [pltpu.make_async_copy(h.at[:, at], v.at[j], in_sem.at[j, i])
                for i, (h, v) in enumerate(((e_h, ev), (oc_h, ocv), (ou_h, ouv)))]

    for j in range(8):
        for c in loads(j):
            c.start()

    for j in range(8):
        for c in loads(j):
            c.wait()

        def group(grp, carry, j=j):
            gmin, lmin, gmax = [], [], []
            for c in range(8):
                gs, ls = [], []
                for h in range(2):
                    r = pl.multiple_of(grp * 128 + 16 * c + 8 * h, 8)
                    oc = ocv[j, pl.ds(r, 8), :] == 1
                    ou = ouv[j, pl.ds(r, 8), :] == 1
                    g = jnp.where(oc, F32(0.0), ev[j, pl.ds(r, 8), :])
                    lk = jnp.where(oc | ou, g, F32(HUGE))
                    gl[0, j, pl.ds(r + 8, 8), :] = g
                    gl[1, j, pl.ds(r + 8, 8), :] = lk
                    gs.append(g)
                    ls.append(lk)
                gmin.append(jnp.minimum(*gs))
                lmin.append(jnp.minimum(*ls))
                gmax.append(jnp.maximum(*gs))
            at = pl.ds(pl.multiple_of(grp * 8, 8), 8)
            ca[0, j, at, :] = tree(gmin, (4, 2, 1), 0, sub, jnp.minimum)
            ca[1, j, at, :] = tree(lmin, (4, 2, 1), 0, sub, jnp.minimum)
            ca[2, j, at, :] = tree(gmax, (4, 2, 1), 0, sub, jnp.maximum)
            return carry

        lax.fori_loop(0, 4, group, 0)

    pl.semaphore_wait(barrier, 8)

    def copy(i, src, dst, d):
        return pltpu.make_async_remote_copy(src_ref=src, dst_ref=dst, send_sem=send.at[i], recv_sem=recv.at[i],
                                            device_id=to[d], device_id_type=MESH)

    copies = [None] * 16
    copies[N_] = copy(N_, gl.at[:, :, pl.ds(8, 8), :], halo.at[1], N_)
    copies[S_] = copy(S_, gl.at[:, :, pl.ds(512, 8), :], halo.at[0], S_)
    copies[N_].start()
    copies[S_].start()

    index = jnp.where((lane >= 8) & (lane < 72), 16 * ((lane - 8) & 7) + 2 * ((lane - 8) >> 3), 0)
    for a in range(3):
        op = jnp.maximum if a == 2 else jnp.minimum
        for grp in range(4):
            x = tree([ca[a, j, pl.ds(8 * grp, 8), :] for j in range(8)], (8, 4, 2), 1, lane, op)
            x = op(x, pltpu.roll(x, 127, 1))
            cp[a, pl.ds(8 * grp, 8), :] = jnp.take_along_axis(x, index, axis=1)
    for grp in range(4):
        at = pl.ds(8 * grp, 8)
        pk[at, :] = jnp.where(((lane >= 8) & (lane < 16)) | ((lane >= 64) & (lane < 72)), cp[0, at, :],
                              jnp.where(((lane >= 16) & (lane < 24)) | ((lane >= 72) & (lane < 80)),
                                        pltpu.roll(cp[1, at, :], 8, 1), pltpu.roll(cp[2, at, :], 16, 1)))
    top, bottom = pl.ds(0, 8), pl.ds(24, 8)
    copies[8 + N_] = copy(8 + N_, cp.at[:, top, :], cn.at[1], N_)
    copies[8 + S_] = copy(8 + S_, cp.at[:, bottom, :], cn.at[0], S_)
    copies[8 + W_] = copy(8 + W_, pk, pwe.at[1, pl.ds(8, 32), :], W_)
    copies[8 + E_] = copy(8 + E_, pk, pwe.at[0, pl.ds(8, 32), :], E_)
    copies[8 + NW_] = copy(8 + NW_, pk.at[top, :], pwe.at[1, pl.ds(40, 8), :], NW_)
    copies[8 + NE_] = copy(8 + NE_, pk.at[top, :], pwe.at[0, pl.ds(40, 8), :], NE_)
    copies[8 + SW_] = copy(8 + SW_, pk.at[bottom, :], pwe.at[1, pl.ds(0, 8), :], SW_)
    copies[8 + SE_] = copy(8 + SE_, pk.at[bottom, :], pwe.at[0, pl.ds(0, 8), :], SE_)
    for i in (NW_, NE_, SW_, SE_, W_, E_, N_, S_):
        copies[8 + i].start()

    for arr in range(2):
        for grp in range(5):
            parts = []
            for i in range(8):
                k = min(8 * grp + i, K - 1)
                for s in (0, 8):
                    at = pl.ds(k + K * s, 8, stride=K)
                    parts.append(jnp.where(lane < 64, gl[arr, 0, at, :], gl[arr, 7, at, :]))
            t = jnp.concatenate(parts, axis=0).T
            fs[0, arr, grp, :, :] = t[0:8, :]
            fs[1, arr, grp, :, :] = t[120:128, :]
        for side in range(2):
            cs[side, 0, arr, :, :] = pltpu.roll(fs[side, arr, 1, :, :], 31, 1)
            cs[side, 1, arr, :, :] = pltpu.roll(
                jnp.where(lane == 15, fs[side, arr, 3, :, :], fs[side, arr, 2, :, :]), 97, 1)
    copies[W_] = copy(W_, fs.at[0], fr.at[1], W_)
    copies[E_] = copy(E_, fs.at[1], fr.at[0], E_)
    copies[NW_] = copy(NW_, cs.at[0, 0], cr.at[1, 1], NW_)
    copies[NE_] = copy(NE_, cs.at[1, 0], cr.at[0, 1], NE_)
    copies[SW_] = copy(SW_, cs.at[0, 1], cr.at[1, 0], SW_)
    copies[SE_] = copy(SE_, cs.at[1, 1], cr.at[0, 0], SE_)
    for i in (NW_, NE_, SW_, SE_, W_, E_):
        copies[i].start()

    def turn(i, carry):
        for u in range(3):
            k = 3 * i + u
            for arr in range(2):
                parts = [gl[arr, j, pl.ds(k + K * s, 8, stride=K), :] for j in range(8) for s in (0, 8)]
                tt[arr, k, pl.ds(8, 128), :] = jnp.concatenate(parts, axis=0).T
        return carry

    lax.fori_loop(0, K // 3, turn, 0)

    for i in range(8):
        copies[i].wait()
    strip = lane & 15
    for arr in range(2):
        parts = []
        for j in range(8):
            parts.append(jnp.where(north, F32(HUGE), halo[0, arr, j, :, :]))
            parts.append(jnp.where(south, F32(HUGE), halo[1, arr, j, :, :]))
        ht[arr, :, :] = jnp.concatenate(parts, axis=0).T
    for arr in range(2):
        for k in range(8):
            for i in range(16):
                at = pl.ds(8 + 8 * i, 8)
                h = ht[arr, pl.ds(8 * i, 8), :]
                tt[arr, k, at, :] = jnp.where(strip == 0, pltpu.roll(h, (128 - k) % 128, 1), tt[arr, k, at, :])
                kk = k + 25
                tt[arr, kk, at, :] = jnp.where(strip == 15, pltpu.roll(h, 32 - kk, 1), tt[arr, kk, at, :])
        edge = []
        for side in range(2):
            up = jnp.where(north, F32(HUGE), cr[side, 0, arr, :, :])
            down = jnp.where(south, F32(HUGE), cr[side, 1, arr, :, :])
            e = [fr[side, arr, grp, :, :] for grp in range(5)]
            e[0] = jnp.where(strip == 0, up, e[0])
            e[3] = jnp.where((strip == 15) & (lane >= 31), down, e[3])
            e[4] = jnp.where(lane == 15, down, e[4])
            edge.append(e)
        for k in range(K):
            i = k % 8
            own = pltpu.roll(tt[arr, k, pl.ds(128, 8), :], 16, 1)
            got = pltpu.roll(edge[0][k // 8], (128 - 16 * i) % 128, 1)
            tt[arr, k, pl.ds(0, 8), :] = jnp.where(lane < 16, got, own)
            own = pltpu.roll(tt[arr, k, pl.ds(8, 8), :], 112, 1)
            got = pltpu.roll(edge[1][k // 8], (112 - 16 * i) % 128, 1)
            tt[arr, k, pl.ds(136, 8), :] = jnp.where(lane >= 112, got, own)

    for i in range(8):
        copies[8 + i].wait()
    ext = []
    for a in range(3):
        tiles = []
        for t in range(6):
            at = pl.ds(8 * t, 8)
            ring = pltpu.roll(jnp.where(lane < 64, pwe[1, at, :], pwe[0, at, :]), 64 - 8 * a, 1)
            mid = cn[0, a, :, :] if t == 0 else cn[1, a, :, :] if t == 5 else cp[a, pl.ds(8 * t - 8, 8), :]
            x = jnp.where((lane >= 8) & (lane < 72), mid, ring)
            if t == 0:
                x = jnp.where(north, F32(HUGE), x)
            if t == 5:
                x = jnp.where(south, F32(HUGE), x)
            tiles.append(x)
        ext.append(tiles)
    gc, kc, v = ext
    for _ in range(4):
        h = [jnp.minimum(jnp.minimum(pltpu.roll(x, 1, 1), pltpu.roll(x, 127, 1)), x) for x in v]
        up = [pltpu.roll(x, 1, 0) for x in h]
        down = [pltpu.roll(x, 7, 0) for x in h]
        new = []
        for t in range(6):
            u = jnp.where(sub == 0, up[t - 1], up[t])
            d = jnp.where(sub == 7, down[(t + 1) % 6], down[t])
            m = jnp.minimum(jnp.minimum(u, d), h[t])
            new.append(jnp.minimum(jnp.maximum(gc[t], jnp.minimum(v[t], m + COARSE_STEP)), kc[t]))
        v = new
    turned = jnp.concatenate(v + [v[0]] * 10, axis=0).T
    cf[...] = turned
    for d in range(4):
        idx = 2 * strip + 7 + d
        for t in range(10):
            at = pl.ds(8 * t, 8)
            zz[d, at, :] = jnp.take_along_axis(cf[at, :], idx, axis=1)
    for d in range(4):
        for t in range(2):
            y = zz[d, pl.ds(7 + 8 * t, 8), :]
            for j in range(1, 8):
                y = jnp.where((lane >> 4) == j, zz[d, pl.ds(7 + 8 * j + 8 * t, 8), :], y)
            yy[d, pl.ds(8 * t, 8), :] = y

    def begin(k, carry):
        d = (k + strip + 8) >> 4
        for t in range(2):
            at = pl.ds(8 * t, 8)
            xb[k, at, :] = jnp.where(d == 0, yy[0, at, :], jnp.where(d == 1, yy[1, at, :],
                                                                     jnp.where(d == 2, yy[2, at, :], yy[3, at, :])))
        return carry

    lax.fori_loop(0, K, begin, 0, unroll=3)

    def begin2(k, carry):
        for t in range(A):
            at = pl.ds(8 * t, 8)
            b = 0 if t == 0 else (t + 1) // 2
            x = xb[k, pl.ds(b, 8, stride=0), :]
            va[k + 1, at, :] = jnp.minimum(jnp.maximum(tt[0, k, at, :], x), tt[1, k, at, :])
        return carry

    lax.fori_loop(0, K, begin2, 0, unroll=3)
    for t in range(A):
        at = pl.ds(8 * t, 8)
        va[0, at, :] = pltpu.roll(va[K, at, :], 1, 1)
        va[K + 1, at, :] = pltpu.roll(va[1, at, :], 127, 1)

    def two(i, carry):
        sweep(va, vb, tt.at[0])
        sweep(vb, va, tt.at[0])
        return carry

    lax.fori_loop(0, 4, two, 0)

    def back(i, carry):
        for u in range(3):
            k = 3 * i + u
            t = va[k + 1, pl.ds(8, 128), :].T
            for j in range(8):
                for h in range(2):
                    ov[j, pl.ds(k + K * 8 * h, 8, stride=K), :] = t[16 * j + 8 * h : 16 * j + 8 * h + 8, :]
        return carry

    lax.fori_loop(0, K // 3, back, 0)
    outs = [pltpu.make_async_copy(ov.at[j, pl.ds(8, 512), :], o_h.at[:, pl.ds(128 * j, 128)], out_sem.at[j])
            for j in range(8)]
    for c in outs:
        c.start()
    for c in outs:
        c.wait()


def solution(mesh):
    rows, cols = mesh.shape["row"], mesh.shape["col"]

    def shards(elevation, ocean, outlet):
        scratch = [
            pltpu.VMEM((8, 512, 128), F32),
            pltpu.VMEM((8, 512, 128), jnp.int32),
            pltpu.VMEM((8, 512, 128), jnp.int32),
            pltpu.VMEM((2, 8, 528, 128), F32),
            pltpu.VMEM((2, 2, 8, 8, 128), F32),
            pltpu.VMEM((2, K, W, 128), F32),
            pltpu.VMEM((K + 2, W, 128), F32),
            pltpu.VMEM((K + 2, W, 128), F32),
            pltpu.VMEM((8, 528, 128), F32),
            pltpu.VMEM((3, 8, 32, 128), F32),
            pltpu.VMEM((3, 32, 128), F32),
            pltpu.VMEM((32, 128), F32),
            pltpu.VMEM((2, 3, 8, 128), F32),
            pltpu.VMEM((2, 48, 128), F32),
            pltpu.VMEM((128, 128), F32),
            pltpu.VMEM((4, 80, 128), F32),
            pltpu.VMEM((4, 16, 128), F32),
            pltpu.VMEM((K, 16, 128), F32),
            pltpu.VMEM((2, 2, 5, 8, 128), F32),
            pltpu.VMEM((2, 2, 5, 8, 128), F32),
            pltpu.VMEM((2, 2, 2, 8, 128), F32),
            pltpu.VMEM((2, 2, 2, 8, 128), F32),
            pltpu.VMEM((2, 128, 128), F32),
            pltpu.SemaphoreType.DMA((8, 3)),
            pltpu.SemaphoreType.DMA((8,)),
            pltpu.SemaphoreType.DMA((16,)),
            pltpu.SemaphoreType.DMA((16,)),
        ]
        return pl.pallas_call(
            lambda *refs: kernel(rows, cols, *refs),
            out_shape=jax.ShapeDtypeStruct((512, 1024), F32),
            in_specs=[pl.BlockSpec(memory_space=pl.ANY)] * 3,
            out_specs=pl.BlockSpec(memory_space=pl.ANY),
            scratch_shapes=scratch,
            name="fill",
            compiler_params=pltpu.CompilerParams(
                collective_id=0, has_side_effects=True, vmem_limit_bytes=48 << 20
            ),
        )(elevation, ocean, outlet)

    return jax.shard_map(
        shards,
        mesh=mesh,
        in_specs=(P("row", "col"), P("row", "col"), P("row", "col")),
        out_specs=P("row", "col"),
        check_vma=False,
    )
```

```python
import jax
import jax.numpy as jnp
from jax import lax
from jax.experimental import pallas as pl
from jax.experimental.pallas import tpu as pltpu
from jax.sharding import PartitionSpec as P

MESH = pl.DeviceIdType.MESH
HUGE = 1e30
FINE_STEP = 2.0 ** (-10)
COARSE_STEP = 2.0 ** (-6)
F32 = jnp.float32

K = 33
W = 144
A = 18

DIRS = [(-1, 0), (1, 0), (0, -1), (0, 1), (-1, -1), (-1, 1), (1, -1), (1, 1)]
N_, S_, W_, E_, NW_, NE_, SW_, SE_ = range(8)
OPP = [S_, N_, E_, W_, SE_, SW_, NE_, NW_]


def lanes():
    return lax.broadcasted_iota(jnp.int32, (8, 128), 1)


def subs():
    return lax.broadcasted_iota(jnp.int32, (8, 128), 0)


def merge(a, b, w, axis, pos, op):
    size = 8 if axis == 0 else 128
    low = (pos & w) == 0
    p = jnp.where(low, a, b)
    q = jnp.where(low, pltpu.roll(a, size - w, axis), pltpu.roll(b, w, axis))
    return op(p, q)


def tree(xs, ws, axis, pos, op):
    for w in ws:
        half = len(xs) // 2
        xs = [merge(xs[i], xs[i + half], w, axis, pos, op) for i in range(half)]
    return xs[0]


def neighbour(d, rows, cols):
    r = lax.axis_index("row")
    c = lax.axis_index("col")
    return (lax.rem(r + d[0] + rows, rows), lax.rem(c + d[1] + cols, cols))


def sweep(src, dst, g):
    def row(ref, k):
        return [ref[k, pl.ds(a, 8, stride=A), :] for a in range(A)]

    def across(vm):
        before = pltpu.roll(vm[A - 1], 1, 0)
        after = pltpu.roll(vm[0], 7, 0)
        m = [None] * A
        for a in range(0, A, 2):
            q = jnp.minimum(vm[a], vm[a + 1])
            m[a] = jnp.minimum(vm[a - 1] if a else before, q)
            m[a + 1] = jnp.minimum(q, vm[a + 2] if a + 2 < A else after)
        return m

    def put(k, v, m):
        out = []
        for a in range(A):
            x = jnp.maximum(g[k, pl.ds(a, 8, stride=A), :], jnp.minimum(v[a], m[a] + FINE_STEP))
            dst[k + 1, pl.ds(a, 8, stride=A), :] = x
            out.append(x)
        return out

    def pair(k):
        v0, v1, v2, v3 = (row(src, k + i) for i in range(4))
        p = [jnp.minimum(x, y) for x, y in zip(v1, v2)]
        m0 = across([jnp.minimum(x, y) for x, y in zip(v0, p)])
        m1 = across([jnp.minimum(x, y) for x, y in zip(p, v3)])
        return put(k, v1, m0), put(k + 1, v2, m1)

    v0, v1, v2 = (row(src, K - 1 + i) for i in range(3))
    last = put(K - 1, v1, across([jnp.minimum(jnp.minimum(x, y), z) for x, y, z in zip(v0, v1, v2)]))
    for a in range(A):
        dst[0, pl.ds(a, 8, stride=A), :] = pltpu.roll(last[a], 1, 1)
    first, _ = pair(0)
    for a in range(A):
        dst[K + 1, pl.ds(a, 8, stride=A), :] = pltpu.roll(first[a], 127, 1)

    def body(i, c):
        pair(2 + 2 * i)
        return c

    lax.fori_loop(0, (K - 3) // 2, body, 0)


def kernel(rows, cols, e_h, oc_h, ou_h, o_h, ev, ocv, ouv, gl, halo, tt, va, vb, ov, ca, cp, pk, cn, pwe, cf, zz,
           yy, xb, fs, fr, cs, cr, ht, in_sem, out_sem, send, recv):
    lane = lanes()
    sub = subs()
    north = lax.axis_index("row") == 0
    south = lax.axis_index("row") == rows - 1
    to = [neighbour(d, rows, cols) for d in DIRS]

    barrier = pltpu.get_barrier_semaphore()
    for dev in to:
        pl.semaphore_signal(barrier, inc=1, device_id=dev, device_id_type=MESH)

    pieces = [((0, 16), (0, 8)), ((48, 16), (0, 8)), ((16, 32), (0, 1)), ((16, 32), (7, 1)), ((16, 16), (1, 6)), ((32, 16), (1, 6))]

    def loads(p):
        (r, nr), (j, nj) = pieces[p]
        return [pltpu.make_async_copy(h.at[pl.ds(r, nr), pl.ds(j, nj)], v.at[pl.ds(r, nr), pl.ds(j, nj)], in_sem.at[p, i])
                for i, (h, v) in enumerate(((e_h, ev), (oc_h, ocv), (ou_h, ouv)))]

    for p in range(6):
        for c in loads(p):
            c.start()

    def arrived(p):
        for c in loads(p):
            c.wait()

    def group(grp, j):
        gmin, lmin, gmax = [], [], []
        for c in range(8):
            gs, ls = [], []
            for h in range(2):
                r = grp * 16 + 2 * c + h
                oc = ocv[r, j] == 1
                ou = ouv[r, j] == 1
                g = jnp.where(oc, F32(0.0), ev[r, j])
                lk = jnp.where(oc | ou, g, F32(HUGE))
                at = pl.ds(8 * r + 8, 8)
                gl[0, j, at, :] = g
                gl[1, j, at, :] = lk
                gs.append(g)
                ls.append(lk)
            gmin.append(jnp.minimum(*gs))
            lmin.append(jnp.minimum(*ls))
            gmax.append(jnp.maximum(*gs))
        at = pl.ds(grp * 8, 8)
        ca[0, j, at, :] = tree(gmin, (4, 2, 1), 0, sub, jnp.minimum)
        ca[1, j, at, :] = tree(lmin, (4, 2, 1), 0, sub, jnp.minimum)
        ca[2, j, at, :] = tree(gmax, (4, 2, 1), 0, sub, jnp.maximum)

    def groups(grp, lo, hi):
        def body(j, carry):
            group(grp, j)
            return carry

        lax.fori_loop(lo, hi, body, 0, unroll=2)

    arrived(0)
    groups(0, 0, 8)
    arrived(1)
    groups(3, 0, 8)
    for j, p in ((0, 2), (7, 3)):
        arrived(p)
        group(1, j)
        group(2, j)


    def copy(i, src, dst, d):
        return pltpu.make_async_remote_copy(src_ref=src, dst_ref=dst, send_sem=send.at[i], recv_sem=recv.at[i],
                                            device_id=to[d], device_id_type=MESH)

    copies = [None] * 16
    copies[N_] = copy(N_, gl.at[:, :, pl.ds(8, 8), :], halo.at[1], N_)
    copies[S_] = copy(S_, gl.at[:, :, pl.ds(512, 8), :], halo.at[0], S_)

    index = jnp.where((lane >= 8) & (lane < 72), 16 * ((lane - 8) & 7) + 2 * ((lane - 8) >> 3), 0)

    def cells(grp, js):
        out = []
        for a in range(3):
            op = jnp.maximum if a == 2 else jnp.minimum
            x = tree([ca[a, j, pl.ds(8 * grp, 8), :] for j in js], (8, 4, 2), 1, lane, op)
            x = op(x, pltpu.roll(x, 127, 1))
            out.append(jnp.take_along_axis(x, index, axis=1))
        return out

    def keep(grp, x):
        for a in range(3):
            cp[a, pl.ds(8 * grp, 8), :] = x[a]

    for grp in range(4):
        x = cells(grp, range(8) if grp in (0, 3) else (0, 0, 0, 0, 7, 7, 7, 7))
        if grp in (0, 3):
            keep(grp, x)
        pk[pl.ds(8 * grp, 8), :] = jnp.where(
            ((lane >= 8) & (lane < 16)) | ((lane >= 64) & (lane < 72)), x[0],
            jnp.where(((lane >= 16) & (lane < 24)) | ((lane >= 72) & (lane < 80)),
                      pltpu.roll(x[1], 8, 1), pltpu.roll(x[2], 16, 1)))
    top, bottom = pl.ds(0, 8), pl.ds(24, 8)
    copies[8 + N_] = copy(8 + N_, cp.at[:, top, :], cn.at[1], N_)
    copies[8 + S_] = copy(8 + S_, cp.at[:, bottom, :], cn.at[0], S_)
    copies[8 + W_] = copy(8 + W_, pk, pwe.at[1, pl.ds(8, 32), :], W_)
    copies[8 + E_] = copy(8 + E_, pk, pwe.at[0, pl.ds(8, 32), :], E_)
    copies[8 + NW_] = copy(8 + NW_, pk.at[top, :], pwe.at[1, pl.ds(40, 8), :], NW_)
    copies[8 + NE_] = copy(8 + NE_, pk.at[top, :], pwe.at[0, pl.ds(40, 8), :], NE_)
    copies[8 + SW_] = copy(8 + SW_, pk.at[bottom, :], pwe.at[1, pl.ds(0, 8), :], SW_)
    copies[8 + SE_] = copy(8 + SE_, pk.at[bottom, :], pwe.at[0, pl.ds(0, 8), :], SE_)

    for arr in range(2):
        for grp in range(5):
            parts = []
            for i in range(8):
                k = min(8 * grp + i, K - 1)
                for s in (0, 8):
                    at = pl.ds(k + K * s, 8, stride=K)
                    parts.append(jnp.where(lane < 64, gl[arr, 0, at, :], gl[arr, 7, at, :]))
            t = jnp.concatenate(parts, axis=0).T
            fs[0, arr, grp, :, :] = t[0:8, :]
            fs[1, arr, grp, :, :] = t[120:128, :]
        for side in range(2):
            cs[side, 0, arr, :, :] = pltpu.roll(fs[side, arr, 1, :, :], 31, 1)
            cs[side, 1, arr, :, :] = pltpu.roll(
                jnp.where(lane == 15, fs[side, arr, 3, :, :], fs[side, arr, 2, :, :]), 97, 1)
    copies[W_] = copy(W_, fs.at[0], fr.at[1], W_)
    copies[E_] = copy(E_, fs.at[1], fr.at[0], E_)
    copies[NW_] = copy(NW_, cs.at[0, 0], cr.at[1, 1], NW_)
    copies[NE_] = copy(NE_, cs.at[1, 0], cr.at[0, 1], NE_)
    copies[SW_] = copy(SW_, cs.at[0, 1], cr.at[1, 0], SW_)
    copies[SE_] = copy(SE_, cs.at[1, 1], cr.at[0, 0], SE_)
    pl.semaphore_wait(barrier, 8)
    for i in (W_, E_, NW_, NE_, SW_, SE_, N_, S_):
        copies[i].start()
        copies[8 + i].start()

    for grp in (1, 2):
        arrived(3 + grp)
        groups(grp, 1, 7)
    for grp in (1, 2):
        keep(grp, cells(grp, range(8)))

    def turn(i, carry):
        for u in range(3):
            k = 3 * i + u
            for arr in range(2):
                parts = [gl[arr, j, pl.ds(k + K * s, 8, stride=K), :] for j in range(8) for s in (0, 8)]
                tt[arr, k, pl.ds(8, 128), :] = jnp.concatenate(parts, axis=0).T
        return carry

    lax.fori_loop(0, K // 3, turn, 0)

    for arr in range(2):
        for k in range(8, 25):
            tt[arr, k, pl.ds(0, 8), :] = pltpu.roll(tt[arr, k, pl.ds(128, 8), :], 16, 1)
            tt[arr, k, pl.ds(136, 8), :] = pltpu.roll(tt[arr, k, pl.ds(8, 8), :], 112, 1)

    for i in range(16):
        copies[i].wait()
    strip = lane & 15
    for arr in range(2):
        up = [jnp.where(north, F32(HUGE), halo[0, arr, j, :, :]) for j in range(8)]
        down = [pltpu.roll(jnp.where(south, F32(HUGE), halo[1, arr, j, :, :]), 7, 0) for j in range(8)]
        for odd in range(2):
            parts = []
            for j in range(8):
                parts.append(jnp.where((sub & 1) == odd, up[j], down[(j + 7) % 8]))
                parts.append(down[j])
            ht[arr, odd, :, :] = jnp.concatenate(parts, axis=0).T
    for arr in range(2):
        for k in range(8):
            for i in range(16):
                at = pl.ds(8 + 8 * i, 8)
                h = pltpu.roll(ht[arr, k % 2, pl.ds(8 * i, 8), :], (128 - k) % 128, 1)
                tt[arr, k, at, :] = jnp.where(strip == 0, h, tt[arr, k, at, :])
                tt[arr, k + 25, at, :] = jnp.where(strip == 15, h, tt[arr, k + 25, at, :])
        edge = []
        for side in range(2):
            up = jnp.where(north, F32(HUGE), cr[side, 0, arr, :, :])
            down = jnp.where(south, F32(HUGE), cr[side, 1, arr, :, :])
            e = [fr[side, arr, grp, :, :] for grp in range(5)]
            e[0] = jnp.where(strip == 0, up, e[0])
            e[3] = jnp.where((strip == 15) & (lane >= 31), down, e[3])
            e[4] = jnp.where(lane == 15, down, e[4])
            edge.append(e)
        for k in range(K):
            i = k % 8
            inner = 8 <= k < 25
            own = tt[arr, k, pl.ds(0, 8), :] if inner else pltpu.roll(tt[arr, k, pl.ds(128, 8), :], 16, 1)
            got = pltpu.roll(edge[0][k // 8], (128 - 16 * i) % 128, 1)
            tt[arr, k, pl.ds(0, 8), :] = jnp.where(lane < 16, got, own)
            own = tt[arr, k, pl.ds(136, 8), :] if inner else pltpu.roll(tt[arr, k, pl.ds(8, 8), :], 112, 1)
            got = pltpu.roll(edge[1][k // 8], (112 - 16 * i) % 128, 1)
            tt[arr, k, pl.ds(136, 8), :] = jnp.where(lane >= 112, got, own)

    ext = []
    for a in range(3):
        tiles = []
        for t in range(6):
            at = pl.ds(8 * t, 8)
            ring = pltpu.roll(jnp.where(lane < 64, pwe[1, at, :], pwe[0, at, :]), 64 - 8 * a, 1)
            mid = cn[0, a, :, :] if t == 0 else cn[1, a, :, :] if t == 5 else cp[a, pl.ds(8 * t - 8, 8), :]
            x = jnp.where((lane >= 8) & (lane < 72), mid, ring)
            if t == 0:
                x = jnp.where(north, F32(HUGE), x)
            if t == 5:
                x = jnp.where(south, F32(HUGE), x)
            tiles.append(x)
        ext.append(tiles)
    gc, kc, v = ext
    for _ in range(4):
        h = [jnp.minimum(jnp.minimum(pltpu.roll(x, 1, 1), pltpu.roll(x, 127, 1)), x) for x in v]
        up = [pltpu.roll(x, 1, 0) for x in h]
        down = [pltpu.roll(x, 7, 0) for x in h]
        new = []
        for t in range(6):
            u = jnp.where(sub == 0, up[t - 1], up[t])
            d = jnp.where(sub == 7, down[(t + 1) % 6], down[t])
            m = jnp.minimum(jnp.minimum(u, d), h[t])
            new.append(jnp.minimum(jnp.maximum(gc[t], jnp.minimum(v[t], m + COARSE_STEP)), kc[t]))
        v = new
    turned = jnp.concatenate(v + [v[0]] * 10, axis=0).T
    cf[...] = turned
    for d in range(4):
        idx = 2 * strip + 7 + d
        for t in range(10):
            at = pl.ds(8 * t, 8)
            zz[d, at, :] = jnp.take_along_axis(cf[at, :], idx, axis=1)
    for d in range(4):
        for t in range(2):
            y = zz[d, pl.ds(7 + 8 * t, 8), :]
            for j in range(1, 8):
                y = jnp.where((lane >> 4) == j, zz[d, pl.ds(7 + 8 * j + 8 * t, 8), :], y)
            yy[d, pl.ds(8 * t, 8), :] = y

    def begin(k, carry):
        d = (k + strip + 8) >> 4
        for t in range(2):
            at = pl.ds(8 * t, 8)
            xb[k, at, :] = jnp.where(d == 0, yy[0, at, :], jnp.where(d == 1, yy[1, at, :],
                                                                     jnp.where(d == 2, yy[2, at, :], yy[3, at, :])))
        return carry

    lax.fori_loop(0, K, begin, 0, unroll=3)

    def begin2(k, carry):
        for t in range(A):
            at = pl.ds(8 * t, 8)
            b = 0 if t == 0 else (t + 1) // 2
            x = xb[k, pl.ds(b, 8, stride=0), :]
            va[k + 1, at, :] = jnp.minimum(jnp.maximum(tt[0, k, at, :], x), tt[1, k, at, :])
        return carry

    lax.fori_loop(0, K, begin2, 0, unroll=3)
    for t in range(A):
        at = pl.ds(8 * t, 8)
        va[0, at, :] = pltpu.roll(va[K, at, :], 1, 1)
        va[K + 1, at, :] = pltpu.roll(va[1, at, :], 127, 1)

    def two(i, carry):
        sweep(va, vb, tt.at[0])
        sweep(vb, va, tt.at[0])
        return carry

    lax.fori_loop(0, 4, two, 0)

    def back(i, carry):
        for u in range(11):
            k = 11 * i + u
            t = va[k + 1, pl.ds(8, 128), :].T
            for j in range(8):
                for h in range(2):
                    ov[j, pl.ds(k + K * 8 * h, 8, stride=K), :] = t[16 * j + 8 * h : 16 * j + 8 * h + 8, :]
        return carry

    lax.fori_loop(0, K // 11, back, 0)
    outs = [pltpu.make_async_copy(ov.at[j, pl.ds(8, 512), :], o_h.at[:, pl.ds(128 * j, 128)], out_sem.at[j])
            for j in range(8)]
    for c in outs:
        c.start()
    for c in outs:
        c.wait()


def tiled(x):
    return x.reshape(64, 8, 8, 128).transpose(0, 2, 1, 3)


def solution(mesh):
    rows, cols = mesh.shape["row"], mesh.shape["col"]

    def shards(elevation, ocean, outlet):
        scratch = [
            pltpu.VMEM((64, 8, 8, 128), F32),
            pltpu.VMEM((64, 8, 8, 128), jnp.int32),
            pltpu.VMEM((64, 8, 8, 128), jnp.int32),
            pltpu.VMEM((2, 8, 528, 128), F32),
            pltpu.VMEM((2, 2, 8, 8, 128), F32),
            pltpu.VMEM((2, K, W, 128), F32),
            pltpu.VMEM((K + 2, W, 128), F32),
            pltpu.VMEM((K + 2, W, 128), F32),
            pltpu.VMEM((8, 528, 128), F32),
            pltpu.VMEM((3, 8, 32, 128), F32),
            pltpu.VMEM((3, 32, 128), F32),
            pltpu.VMEM((32, 128), F32),
            pltpu.VMEM((2, 3, 8, 128), F32),
            pltpu.VMEM((2, 48, 128), F32),
            pltpu.VMEM((128, 128), F32),
            pltpu.VMEM((4, 80, 128), F32),
            pltpu.VMEM((4, 16, 128), F32),
            pltpu.VMEM((K, 16, 128), F32),
            pltpu.VMEM((2, 2, 5, 8, 128), F32),
            pltpu.VMEM((2, 2, 5, 8, 128), F32),
            pltpu.VMEM((2, 2, 2, 8, 128), F32),
            pltpu.VMEM((2, 2, 2, 8, 128), F32),
            pltpu.VMEM((2, 2, 128, 128), F32),
            pltpu.SemaphoreType.DMA((6, 3)),
            pltpu.SemaphoreType.DMA((8,)),
            pltpu.SemaphoreType.DMA((16,)),
            pltpu.SemaphoreType.DMA((16,)),
        ]
        return pl.pallas_call(
            lambda *refs: kernel(rows, cols, *refs),
            out_shape=jax.ShapeDtypeStruct((512, 1024), F32),
            in_specs=[pl.BlockSpec(memory_space=pl.ANY)] * 3,
            out_specs=pl.BlockSpec(memory_space=pl.ANY),
            scratch_shapes=scratch,
            name="fill",
            compiler_params=pltpu.CompilerParams(
                collective_id=0, has_side_effects=True, vmem_limit_bytes=50 << 20
            ),
        )(tiled(elevation), tiled(ocean), tiled(outlet))

    return jax.shard_map(
        shards,
        mesh=mesh,
        in_specs=(P("row", "col"), P("row", "col"), P("row", "col")),
        out_specs=P("row", "col"),
        check_vma=False,
    )
```

```python
import jax
import jax.numpy as jnp
from jax import lax
from jax.experimental import pallas as pl
from jax.experimental.pallas import tpu as pltpu
from jax.sharding import PartitionSpec as P

MESH = pl.DeviceIdType.MESH
HUGE = 1e30
FINE_STEP = 2.0 ** (-10)
COARSE_STEP = 2.0 ** (-6)
F32 = jnp.float32

K = 33
W = 144
A = 18

DIRS = [(-1, 0), (1, 0), (0, -1), (0, 1), (-1, -1), (-1, 1), (1, -1), (1, 1)]
N_, S_, W_, E_, NW_, NE_, SW_, SE_ = range(8)
OPP = [S_, N_, E_, W_, SE_, SW_, NE_, NW_]


def lanes():
    return lax.broadcasted_iota(jnp.int32, (8, 128), 1)


def subs():
    return lax.broadcasted_iota(jnp.int32, (8, 128), 0)


def merge(a, b, w, axis, pos, op):
    size = 8 if axis == 0 else 128
    low = (pos & w) == 0
    p = jnp.where(low, a, b)
    q = jnp.where(low, pltpu.roll(a, size - w, axis), pltpu.roll(b, w, axis))
    return op(p, q)


def tree(xs, ws, axis, pos, op):
    for w in ws:
        half = len(xs) // 2
        xs = [merge(xs[i], xs[i + half], w, axis, pos, op) for i in range(half)]
    return xs[0]


def neighbour(d, rows, cols):
    r = lax.axis_index("row")
    c = lax.axis_index("col")
    return (lax.rem(r + d[0] + rows, rows), lax.rem(c + d[1] + cols, cols))


def sweep(src, dst, g):
    def row(ref, k):
        return [ref[k, pl.ds(a, 8, stride=A), :] for a in range(A)]

    def across(vm):
        before = pltpu.roll(vm[A - 1], 1, 0)
        after = pltpu.roll(vm[0], 7, 0)
        m = [None] * A
        for a in range(0, A, 2):
            q = jnp.minimum(vm[a], vm[a + 1])
            m[a] = jnp.minimum(vm[a - 1] if a else before, q)
            m[a + 1] = jnp.minimum(q, vm[a + 2] if a + 2 < A else after)
        return m

    def put(k, v, m):
        out = []
        for a in range(A):
            x = jnp.maximum(g[k, pl.ds(a, 8, stride=A), :], jnp.minimum(v[a], m[a] + FINE_STEP))
            dst[k + 1, pl.ds(a, 8, stride=A), :] = x
            out.append(x)
        return out

    def pair(k):
        v0, v1, v2, v3 = (row(src, k + i) for i in range(4))
        p = [jnp.minimum(x, y) for x, y in zip(v1, v2)]
        m0 = across([jnp.minimum(x, y) for x, y in zip(v0, p)])
        m1 = across([jnp.minimum(x, y) for x, y in zip(p, v3)])
        return put(k, v1, m0), put(k + 1, v2, m1)

    v0, v1, v2 = (row(src, K - 1 + i) for i in range(3))
    last = put(K - 1, v1, across([jnp.minimum(jnp.minimum(x, y), z) for x, y, z in zip(v0, v1, v2)]))
    for a in range(A):
        dst[0, pl.ds(a, 8, stride=A), :] = pltpu.roll(last[a], 1, 1)
    first, _ = pair(0)
    for a in range(A):
        dst[K + 1, pl.ds(a, 8, stride=A), :] = pltpu.roll(first[a], 127, 1)

    def body(i, c):
        pair(2 + 2 * i)
        return c

    lax.fori_loop(0, (K - 3) // 2, body, 0, unroll=3)


def kernel(rows, cols, e_h, oc_h, ou_h, o_h, ev, ocv, ouv, gl, tt, va, vb, ov, ca, cp, cf, zz,
           yy, xb, rs, rr, es, er, ds, dr, ht, in_sem, out_sem, send, recv):
    lane = lanes()
    sub = subs()
    north = lax.axis_index("row") == 0
    south = lax.axis_index("row") == rows - 1
    to = [neighbour(d, rows, cols) for d in DIRS]

    barrier = pltpu.get_barrier_semaphore()
    for i in (NW_, NE_, SW_, SE_, W_, E_, N_, S_):
        pl.semaphore_signal(barrier, inc=1, device_id=to[i], device_id_type=MESH)

    pieces = [((0, 16), (0, 8)), ((48, 16), (0, 8)), ((16, 32), (0, 1)), ((16, 32), (7, 1)), ((16, 16), (1, 6)), ((32, 16), (1, 6))]

    def loads(p):
        (r, nr), (j, nj) = pieces[p]
        return [pltpu.make_async_copy(h.at[pl.ds(r, nr), pl.ds(j, nj)], v.at[pl.ds(r, nr), pl.ds(j, nj)], in_sem.at[p, i])
                for i, (h, v) in enumerate(((e_h, ev), (oc_h, ocv), (ou_h, ouv)))]

    for p in range(6):
        for c in loads(p):
            c.start()

    def arrived(p):
        for c in loads(p):
            c.wait()

    def group(grp, j):
        gmin, lmin, gmax = [], [], []
        for c in range(8):
            gs, ls = [], []
            for h in range(2):
                r = grp * 16 + 2 * c + h
                oc = ocv[r, j] == 1
                ou = ouv[r, j] == 1
                g = jnp.where(oc, F32(0.0), ev[r, j])
                lk = jnp.where(oc | ou, g, F32(HUGE))
                at = pl.ds(8 * r + 8, 8)
                gl[0, j, at, :] = g
                gl[1, j, at, :] = lk
                gs.append(g)
                ls.append(lk)
            gmin.append(jnp.minimum(*gs))
            lmin.append(jnp.minimum(*ls))
            gmax.append(jnp.maximum(*gs))
        at = pl.ds(grp * 8, 8)
        ca[0, j, at, :] = tree(gmin, (4, 2, 1), 0, sub, jnp.minimum)
        ca[1, j, at, :] = tree(lmin, (4, 2, 1), 0, sub, jnp.minimum)
        ca[2, j, at, :] = tree(gmax, (4, 2, 1), 0, sub, jnp.maximum)

    def groups(grp, lo, hi):
        def body(j, carry):
            group(grp, j)
            return carry

        lax.fori_loop(lo, hi, body, 0, unroll=2)

    arrived(0)
    groups(0, 0, 8)
    arrived(1)
    groups(3, 0, 8)
    for j, p in ((0, 2), (7, 3)):
        arrived(p)
        group(1, j)
        group(2, j)


    def copy(d, src, dst):
        return pltpu.make_async_remote_copy(src_ref=src, dst_ref=dst, send_sem=send.at[d], recv_sem=recv.at[d],
                                            device_id=to[d], device_id_type=MESH)

    copies = [copy(N_, rs.at[0], rr.at[1]), copy(S_, rs.at[1], rr.at[0]),
              copy(W_, es.at[0], er.at[1]), copy(E_, es.at[1], er.at[0]),
              copy(NW_, ds.at[0, 0], dr.at[1, 1]), copy(NE_, ds.at[1, 0], dr.at[0, 1]),
              copy(SW_, ds.at[0, 1], dr.at[1, 0]), copy(SE_, ds.at[1, 1], dr.at[0, 0])]
    for arr in range(2):
        for j in range(8):
            rs[0, 8 * arr + j] = gl[arr, j, pl.ds(8, 8), :]
            rs[1, 8 * arr + j] = gl[arr, j, pl.ds(512, 8), :]

    index = jnp.where((lane >= 8) & (lane < 72), 16 * ((lane - 8) & 7) + 2 * ((lane - 8) >> 3), 0)

    def cells(grp, js):
        out = []
        for a in range(3):
            op = jnp.maximum if a == 2 else jnp.minimum
            x = tree([ca[a, j, pl.ds(8 * grp, 8), :] for j in js], (8, 4, 2), 1, lane, op)
            x = op(x, pltpu.roll(x, 127, 1))
            out.append(jnp.take_along_axis(x, index, axis=1))
        return out

    def keep(grp, x):
        for a in range(3):
            cp[a, pl.ds(8 * grp, 8), :] = x[a]

    packs = []
    for grp in range(4):
        x = cells(grp, range(8) if grp in (0, 3) else (0, 0, 0, 0, 7, 7, 7, 7))
        if grp in (0, 3):
            keep(grp, x)
            for a in range(3):
                rs[grp // 3, 16 + a] = x[a]
        pk = jnp.where(
            ((lane >= 8) & (lane < 16)) | ((lane >= 64) & (lane < 72)), x[0],
            jnp.where(((lane >= 16) & (lane < 24)) | ((lane >= 72) & (lane < 80)),
                      pltpu.roll(x[1], 8, 1), pltpu.roll(x[2], 16, 1)))
        packs.append(pk)
        for side in range(2):
            if grp in (0, 3):
                ds[side, grp // 3, 1] = pk
    ends = [[None] * 5, [None] * 5]
    for arr in range(2):
        for grp in range(5):
            parts = []
            for i in range(8):
                k = min(8 * grp + i, K - 1)
                for s in (0, 8):
                    at = pl.ds(k + K * s, 8, stride=K)
                    parts.append(jnp.where(lane < 64, gl[arr, 0, at, :], gl[arr, 7, at, :]))
            t = jnp.concatenate(parts, axis=0).T
            ends[arr][grp] = (t[0:8, :], t[120:128, :])
            for side in range(2):
                if grp < 4:
                    es[side, 4 * arr + grp] = ends[arr][grp][side]
    strip = lane & 15
    for side in range(2):
        x = jnp.where(lane < 16, ends[0][4][side], pltpu.roll(ends[1][4][side], 16, 1))
        for t in range(4):
            y = pltpu.roll(packs[t], (24 * t + (24 if side == 0 else 96)) % 128, 1)
            x = jnp.where(lane < 32 + 24 * t, x, y)
        es[side, 8] = x
        g, lk = (pltpu.roll(ends[arr][1][side], 31 + arr, 1) for arr in range(2))
        ds[side, 0, 0] = jnp.where(strip == 15, g, lk)
        g, lk = (pltpu.roll(jnp.where(lane == 15, ends[arr][3][side], ends[arr][2][side]), 97 + arr, 1) for arr in range(2))
        ds[side, 1, 0] = jnp.where(strip == 0, g, lk)
    pl.semaphore_wait(barrier, 8)
    for i in (W_, E_, NW_, NE_, SW_, SE_, N_, S_):
        copies[i].start()

    for grp in (1, 2):
        arrived(3 + grp)
        groups(grp, 1, 7)
    for grp in (1, 2):
        keep(grp, cells(grp, range(8)))

    def turn(i, carry):
        for u in range(3):
            k = 3 * i + u
            for arr in range(2):
                parts = [gl[arr, j, pl.ds(k + K * s, 8, stride=K), :] for j in range(8) for s in (0, 8)]
                tt[arr, k, pl.ds(8, 128), :] = jnp.concatenate(parts, axis=0).T
        return carry

    lax.fori_loop(0, K // 3, turn, 0)

    for arr in range(2):
        for k in range(8, 25):
            tt[arr, k, pl.ds(0, 8), :] = pltpu.roll(tt[arr, k, pl.ds(128, 8), :], 16, 1)
            tt[arr, k, pl.ds(136, 8), :] = pltpu.roll(tt[arr, k, pl.ds(8, 8), :], 112, 1)

    for i in range(8):
        copies[i].wait()
    for arr in range(2):
        up = [jnp.where(north, F32(HUGE), rr[0, 8 * arr + j]) for j in range(8)]
        down = [pltpu.roll(jnp.where(south, F32(HUGE), rr[1, 8 * arr + j]), 7, 0) for j in range(8)]
        for odd in range(2):
            parts = []
            for j in range(8):
                parts.append(jnp.where((sub & 1) == odd, up[j], down[(j + 7) % 8]))
                parts.append(down[j])
            ht[arr, odd, :, :] = jnp.concatenate(parts, axis=0).T
    for arr in range(2):
        for k in range(8):
            for i in range(16):
                at = pl.ds(8 + 8 * i, 8)
                h = pltpu.roll(ht[arr, k % 2, pl.ds(8 * i, 8), :], (128 - k) % 128, 1)
                tt[arr, k, at, :] = jnp.where(strip == 0, h, tt[arr, k, at, :])
                tt[arr, k + 25, at, :] = jnp.where(strip == 15, h, tt[arr, k + 25, at, :])
        edge = []
        for side in range(2):
            corner = [pltpu.roll(dr[side, i, 0], 127, 1) if arr else dr[side, i, 0] for i in range(2)]
            up = jnp.where(north, F32(HUGE), corner[0])
            down = jnp.where(south, F32(HUGE), corner[1])
            e = [er[side, 4 * arr + grp] for grp in range(4)]
            e.append(pltpu.roll(er[side, 8], 112, 1) if arr else er[side, 8])
            e[0] = jnp.where(strip == 0, up, e[0])
            e[3] = jnp.where((strip == 15) & (lane >= 31), down, e[3])
            e[4] = jnp.where(lane == 15, down, e[4])
            edge.append(e)
        for k in range(K):
            i = k % 8
            inner = 8 <= k < 25
            own = tt[arr, k, pl.ds(0, 8), :] if inner else pltpu.roll(tt[arr, k, pl.ds(128, 8), :], 16, 1)
            got = pltpu.roll(edge[0][k // 8], (128 - 16 * i) % 128, 1)
            tt[arr, k, pl.ds(0, 8), :] = jnp.where(lane < 16, got, own)
            own = tt[arr, k, pl.ds(136, 8), :] if inner else pltpu.roll(tt[arr, k, pl.ds(8, 8), :], 112, 1)
            got = pltpu.roll(edge[1][k // 8], (112 - 16 * i) % 128, 1)
            tt[arr, k, pl.ds(136, 8), :] = jnp.where(lane >= 112, got, own)

    rings = []
    for t in range(6):
        if t in (0, 5):
            west, east = (dr[i, t // 5, 1] for i in range(2))
        else:
            west, east = (pltpu.roll(er[i, 8], (b - 24 * t + 24) % 128, 1) for i, b in ((0, 32), (1, 104)))
        rings.append(jnp.where(lane < 64, east, west))
    ext = []
    for a in range(3):
        tiles = []
        for t in range(6):
            ring = pltpu.roll(rings[t], 64 - 8 * a, 1)
            mid = rr[0, 16 + a] if t == 0 else rr[1, 16 + a] if t == 5 else cp[a, pl.ds(8 * t - 8, 8), :]
            x = jnp.where((lane >= 8) & (lane < 72), mid, ring)
            if t == 0:
                x = jnp.where(north, F32(HUGE), x)
            if t == 5:
                x = jnp.where(south, F32(HUGE), x)
            tiles.append(x)
        ext.append(tiles)
    gc, kc, v = ext
    for _ in range(4):
        h = [jnp.minimum(jnp.minimum(pltpu.roll(x, 1, 1), pltpu.roll(x, 127, 1)), x) for x in v]
        up = [pltpu.roll(x, 1, 0) for x in h]
        down = [pltpu.roll(x, 7, 0) for x in h]
        new = []
        for t in range(6):
            u = jnp.where(sub == 0, up[t - 1], up[t])
            d = jnp.where(sub == 7, down[(t + 1) % 6], down[t])
            m = jnp.minimum(jnp.minimum(u, d), h[t])
            new.append(jnp.minimum(jnp.maximum(gc[t], jnp.minimum(v[t], m + COARSE_STEP)), kc[t]))
        v = new
    turned = jnp.concatenate(v + [v[0]] * 10, axis=0).T
    cf[...] = turned
    for d in range(4):
        idx = 2 * strip + 7 + d
        for t in range(10):
            at = pl.ds(8 * t, 8)
            zz[d, at, :] = jnp.take_along_axis(cf[at, :], idx, axis=1)
    for d in range(4):
        for t in range(2):
            y = zz[d, pl.ds(7 + 8 * t, 8), :]
            for j in range(1, 8):
                y = jnp.where((lane >> 4) == j, zz[d, pl.ds(7 + 8 * j + 8 * t, 8), :], y)
            yy[d, pl.ds(8 * t, 8), :] = y

    def begin(k, carry):
        d = (k + strip + 8) >> 4
        for t in range(2):
            at = pl.ds(8 * t, 8)
            xb[k, at, :] = jnp.where(d == 0, yy[0, at, :], jnp.where(d == 1, yy[1, at, :],
                                                                     jnp.where(d == 2, yy[2, at, :], yy[3, at, :])))
        return carry

    lax.fori_loop(0, K, begin, 0, unroll=3)

    def begin2(k, carry):
        for t in range(A):
            at = pl.ds(8 * t, 8)
            b = 0 if t == 0 else (t + 1) // 2
            x = xb[k, pl.ds(b, 8, stride=0), :]
            va[k + 1, at, :] = jnp.minimum(jnp.maximum(tt[0, k, at, :], x), tt[1, k, at, :])
        return carry

    lax.fori_loop(0, K, begin2, 0, unroll=3)
    for t in range(A):
        at = pl.ds(8 * t, 8)
        va[0, at, :] = pltpu.roll(va[K, at, :], 1, 1)
        va[K + 1, at, :] = pltpu.roll(va[1, at, :], 127, 1)

    def two(i, carry):
        sweep(va, vb, tt.at[0])
        sweep(vb, va, tt.at[0])
        return carry

    lax.fori_loop(0, 4, two, 0)

    def back(i, carry):
        for u in range(11):
            k = 11 * i + u
            t = va[k + 1, pl.ds(8, 128), :].T
            for j in range(8):
                for h in range(2):
                    ov[j, pl.ds(k + K * 8 * h, 8, stride=K), :] = t[16 * j + 8 * h : 16 * j + 8 * h + 8, :]
        return carry

    lax.fori_loop(0, K // 11, back, 0)
    outs = [pltpu.make_async_copy(ov.at[j, pl.ds(8, 512), :], o_h.at[:, pl.ds(128 * j, 128)], out_sem.at[j])
            for j in range(8)]
    for c in outs:
        c.start()
    for c in outs:
        c.wait()


def tiled(x):
    return x.reshape(64, 8, 8, 128).transpose(0, 2, 1, 3)


def solution(mesh):
    rows, cols = mesh.shape["row"], mesh.shape["col"]

    def shards(elevation, ocean, outlet):
        scratch = [
            pltpu.VMEM((64, 8, 8, 128), F32),
            pltpu.VMEM((64, 8, 8, 128), jnp.int32),
            pltpu.VMEM((64, 8, 8, 128), jnp.int32),
            pltpu.VMEM((2, 8, 528, 128), F32),
            pltpu.VMEM((2, K, W, 128), F32),
            pltpu.VMEM((K + 2, W, 128), F32),
            pltpu.VMEM((K + 2, W, 128), F32),
            pltpu.VMEM((8, 528, 128), F32),
            pltpu.VMEM((3, 8, 32, 128), F32),
            pltpu.VMEM((3, 32, 128), F32),
            pltpu.VMEM((128, 128), F32),
            pltpu.VMEM((4, 80, 128), F32),
            pltpu.VMEM((4, 16, 128), F32),
            pltpu.VMEM((K, 16, 128), F32),
            pltpu.VMEM((2, 19, 8, 128), F32),
            pltpu.VMEM((2, 19, 8, 128), F32),
            pltpu.VMEM((2, 9, 8, 128), F32),
            pltpu.VMEM((2, 9, 8, 128), F32),
            pltpu.VMEM((2, 2, 2, 8, 128), F32),
            pltpu.VMEM((2, 2, 2, 8, 128), F32),
            pltpu.VMEM((2, 2, 128, 128), F32),
            pltpu.SemaphoreType.DMA((6, 3)),
            pltpu.SemaphoreType.DMA((8,)),
            pltpu.SemaphoreType.DMA((8,)),
            pltpu.SemaphoreType.DMA((8,)),
        ]
        return pl.pallas_call(
            lambda *refs: kernel(rows, cols, *refs),
            out_shape=jax.ShapeDtypeStruct((512, 1024), F32),
            in_specs=[pl.BlockSpec(memory_space=pl.ANY)] * 3,
            out_specs=pl.BlockSpec(memory_space=pl.ANY),
            scratch_shapes=scratch,
            name="fill",
            compiler_params=pltpu.CompilerParams(
                collective_id=0, has_side_effects=True, vmem_limit_bytes=50 << 20
            ),
        )(tiled(elevation), tiled(ocean), tiled(outlet))

    return jax.shard_map(
        shards,
        mesh=mesh,
        in_specs=(P("row", "col"), P("row", "col"), P("row", "col")),
        out_specs=P("row", "col"),
        check_vma=False,
    )
```

```python
import jax
import jax.numpy as jnp
from jax import lax
from jax.experimental import pallas as pl
from jax.experimental.pallas import tpu as pltpu
from jax.sharding import PartitionSpec as P

MESH = pl.DeviceIdType.MESH
HUGE = 1e30
FINE_STEP = 2.0 ** (-10)
COARSE_STEP = 2.0 ** (-6)
F32 = jnp.float32

KI, KE, KS = 25, 11, 6
AJ, AS = 18, 11

DIRS = [(-1, 0), (1, 0), (0, -1), (0, 1), (-1, -1), (-1, 1), (1, -1), (1, 1)]
N_, S_, W_, E_, NW_, NE_, SW_, SE_ = range(8)
OPP = [S_, N_, E_, W_, SE_, SW_, NE_, NW_]


def lanes():
    return lax.broadcasted_iota(jnp.int32, (8, 128), 1)


def subs():
    return lax.broadcasted_iota(jnp.int32, (8, 128), 0)


def merge(a, b, w, axis, pos, op):
    size = 8 if axis == 0 else 128
    low = (pos & w) == 0
    p = jnp.where(low, a, b)
    q = jnp.where(low, pltpu.roll(a, size - w, axis), pltpu.roll(b, w, axis))
    return op(p, q)


def tree(xs, ws, axis, pos, op):
    for w in ws:
        half = len(xs) // 2
        xs = [merge(xs[i], xs[i + half], w, axis, pos, op) for i in range(half)]
    return xs[0]


def neighbour(d, rows, cols):
    r = lax.axis_index("row")
    c = lax.axis_index("col")
    return (lax.rem(r + d[0] + rows, rows), lax.rem(c + d[1] + cols, cols))


def sweep(src, dst, g, K, A, loop):
    def row(ref, k):
        return [ref[k, pl.ds(a, 8, stride=A), :] for a in range(A)]

    def across(vm):
        before = pltpu.roll(vm[A - 1], 1, 0)
        after = pltpu.roll(vm[0], 7, 0)
        m = [None] * A
        for a in range(0, A - 1, 2):
            q = jnp.minimum(vm[a], vm[a + 1])
            m[a] = jnp.minimum(vm[a - 1] if a else before, q)
            m[a + 1] = jnp.minimum(q, vm[a + 2] if a + 2 < A else after)
        if A % 2:
            m[A - 1] = jnp.minimum(jnp.minimum(vm[A - 2], vm[A - 1]), after)
        return m

    def put(k, v, m):
        out = []
        for a in range(A):
            x = jnp.maximum(g[k, pl.ds(a, 8, stride=A), :], jnp.minimum(v[a], m[a] + FINE_STEP))
            dst[k + 1, pl.ds(a, 8, stride=A), :] = x
            out.append(x)
        return out

    def pair(k):
        v0, v1, v2, v3 = (row(src, k + i) for i in range(4))
        p = [jnp.minimum(x, y) for x, y in zip(v1, v2)]
        m0 = across([jnp.minimum(x, y) for x, y in zip(v0, p)])
        m1 = across([jnp.minimum(x, y) for x, y in zip(p, v3)])
        return put(k, v1, m0), put(k + 1, v2, m1)

    if K % 2:
        v0, v1, v2 = (row(src, K - 1 + i) for i in range(3))
        last = put(K - 1, v1, across([jnp.minimum(jnp.minimum(x, y), z) for x, y, z in zip(v0, v1, v2)]))
    else:
        last = pair(K - 2)[1]
    for a in range(A):
        dst[0, pl.ds(a, 8, stride=A), :] = pltpu.roll(last[a], 1, 1)
    first, _ = pair(0)
    for a in range(A):
        dst[K + 1, pl.ds(a, 8, stride=A), :] = pltpu.roll(first[a], 127, 1)

    count = (K - 3) // 2 if K % 2 else (K - 4) // 2
    if loop:
        def body(i, c):
            pair(2 + 2 * i)
            return c

        lax.fori_loop(0, count, body, 0)
    else:
        for i in range(count):
            pair(2 + 2 * i)


def kernel(rows, cols, e_h, oc_h, ou_h, o_h, ev, ocv, ouv, gl, ti, te, ts, vi, wi, ve, we, vs, ws, ov, oe, ca, cp, cf, zz,
           yy, xb, cb, rs, rr, es, er, ds, dr, ht, in_sem, out_sem, send, recv):
    lane = lanes()
    sub = subs()
    north = lax.axis_index("row") == 0
    south = lax.axis_index("row") == rows - 1
    to = [neighbour(d, rows, cols) for d in DIRS]

    barrier = pltpu.get_barrier_semaphore()
    for i in (NW_, NE_, SW_, SE_, W_, E_, N_, S_):
        pl.semaphore_signal(barrier, inc=1, device_id=to[i], device_id_type=MESH)

    pieces = [((0, 16), (0, 8)), ((48, 16), (0, 8)), ((16, 32), (0, 1)), ((16, 32), (7, 1)), ((16, 16), (1, 6)), ((32, 16), (1, 6))]

    def loads(p):
        (r, nr), (j, nj) = pieces[p]
        return [pltpu.make_async_copy(h.at[pl.ds(r, nr), pl.ds(j, nj)], v.at[pl.ds(r, nr), pl.ds(j, nj)], in_sem.at[p, i])
                for i, (h, v) in enumerate(((e_h, ev), (oc_h, ocv), (ou_h, ouv)))]

    for p in range(6):
        for c in loads(p):
            c.start()

    def arrived(p):
        for c in loads(p):
            c.wait()

    def group(grp, j):
        gmin, lmin, gmax = [], [], []
        for c in range(8):
            gs, ls = [], []
            for h in range(2):
                r = grp * 16 + 2 * c + h
                oc = ocv[r, j] == 1
                ou = ouv[r, j] == 1
                g = jnp.where(oc, F32(0.0), ev[r, j])
                lk = jnp.where(oc | ou, g, F32(HUGE))
                at = pl.ds(8 * r + 8, 8)
                gl[0, j, at, :] = g
                gl[1, j, at, :] = lk
                gs.append(g)
                ls.append(lk)
            gmin.append(jnp.minimum(*gs))
            lmin.append(jnp.minimum(*ls))
            gmax.append(jnp.maximum(*gs))
        at = pl.ds(grp * 8, 8)
        ca[0, j, at, :] = tree(gmin, (4, 2, 1), 0, sub, jnp.minimum)
        ca[1, j, at, :] = tree(lmin, (4, 2, 1), 0, sub, jnp.minimum)
        ca[2, j, at, :] = tree(gmax, (4, 2, 1), 0, sub, jnp.maximum)

    def groups(grp, lo, hi):
        def body(j, carry):
            group(grp, j)
            return carry

        lax.fori_loop(lo, hi, body, 0, unroll=2)

    arrived(0)
    groups(0, 0, 8)
    arrived(1)
    groups(3, 0, 8)
    for j, p in ((0, 2), (7, 3)):
        arrived(p)
        group(1, j)
        group(2, j)


    def copy(d, src, dst):
        return pltpu.make_async_remote_copy(src_ref=src, dst_ref=dst, send_sem=send.at[d], recv_sem=recv.at[d],
                                            device_id=to[d], device_id_type=MESH)

    copies = [copy(N_, rs.at[0], rr.at[1]), copy(S_, rs.at[1], rr.at[0]),
              copy(W_, es.at[0], er.at[1]), copy(E_, es.at[1], er.at[0]),
              copy(NW_, ds.at[0, 0], dr.at[1, 1]), copy(NE_, ds.at[1, 0], dr.at[0, 1]),
              copy(SW_, ds.at[0, 1], dr.at[1, 0]), copy(SE_, ds.at[1, 1], dr.at[0, 0])]
    for arr in range(2):
        for j in range(8):
            rs[0, 8 * arr + j] = gl[arr, j, pl.ds(8, 8), :]
            rs[1, 8 * arr + j] = gl[arr, j, pl.ds(512, 8), :]

    index = jnp.where((lane >= 8) & (lane < 72), 16 * ((lane - 8) & 7) + 2 * ((lane - 8) >> 3), 0)

    def cells(grp, js):
        out = []
        for a in range(3):
            op = jnp.maximum if a == 2 else jnp.minimum
            x = tree([ca[a, j, pl.ds(8 * grp, 8), :] for j in js], (8, 4, 2), 1, lane, op)
            x = op(x, pltpu.roll(x, 127, 1))
            out.append(jnp.take_along_axis(x, index, axis=1))
        return out

    def keep(grp, x):
        for a in range(3):
            cp[a, pl.ds(8 * grp, 8), :] = x[a]

    packs = []
    for grp in range(4):
        x = cells(grp, range(8) if grp in (0, 3) else (0, 0, 0, 0, 7, 7, 7, 7))
        if grp in (0, 3):
            keep(grp, x)
            for a in range(3):
                rs[grp // 3, 16 + a] = x[a]
        pk = jnp.where(
            ((lane >= 8) & (lane < 16)) | ((lane >= 64) & (lane < 72)), x[0],
            jnp.where(((lane >= 16) & (lane < 24)) | ((lane >= 72) & (lane < 80)),
                      pltpu.roll(x[1], 8, 1), pltpu.roll(x[2], 16, 1)))
        packs.append(pk)
        for side in range(2):
            if grp in (0, 3):
                ds[side, grp // 3, 1] = pk
    strip = lane & 15

    def ends_at(k):
        return [pl.ds(k, 8, stride=KE), pl.ds(440 + k, 8, stride=KE)]

    def sides_at(k):
        return [pl.ds(72 + 8 * KS * m + k, 8, stride=KS) for m in range(8)]

    def outer(arr, at):
        return jnp.where(lane < 64, gl[arr, 0, at, :], gl[arr, 7, at, :])

    def edges_of(arr, ats):
        t = jnp.concatenate([outer(arr, at) for at in ats], axis=0).T
        return t[0:8, :], t[120:128, :]

    rest = []
    corners = []
    for arr in range(2):
        first8 = edges_of(arr, [at for k in range(8) for at in ends_at(k)])
        rest.append(edges_of(arr, [at for k in range(8, 16) for at in ends_at(min(k, KE - 1))]))
        for side in range(2):
            es[side, arr] = first8[side]
        for p in range(3):
            x = edges_of(arr, sides_at(2 * p) + sides_at(2 * p + 1))
            for side in range(2):
                es[side, 2 + 3 * arr + p] = x[side]
        cb[arr, pl.ds(0, 8, stride=16), :] = outer(arr, pl.ds(512, 8))
        cb[arr, pl.ds(15, 8, stride=16), :] = pltpu.roll(outer(arr, pl.ds(8, 8)), 3, 0)
        t = cb[arr].T
        corners.append((t[0:8, :], t[120:128, :]))
    for side in range(2):
        x = packs[0]
        for t in range(4):
            y = pltpu.roll(packs[t], (24 * t + (24 if side == 0 else 96)) % 128, 1)
            x = jnp.where(lane < 32 + 24 * t, x, y)
        es[side, 8] = x
        es[side, 9] = jnp.where(lane < 48, rest[0][side], pltpu.roll(rest[1][side], 48, 1))
        x = jnp.where((strip == 0) | (strip == 15), corners[0][side], pltpu.roll(corners[1][side], 2, 1))
        ds[side, 0, 0] = x
        ds[side, 1, 0] = x

    def turn(dst, arr, k, ats):
        parts = [gl[arr, j, at, :] for j in range(8) for at in ats]
        dst[arr, k, pl.ds(8, 128), :] = jnp.concatenate(parts, axis=0).T

    def coarse_sweeps(gc, kc, v):
        for _ in range(4):
            h = [jnp.minimum(jnp.minimum(pltpu.roll(x, 1, 1), pltpu.roll(x, 127, 1)), x) for x in v]
            up = [pltpu.roll(x, 1, 0) for x in h]
            down = [pltpu.roll(x, 7, 0) for x in h]
            new = []
            for t in range(6):
                u = jnp.where(sub == 0, up[t - 1], up[t])
                d = jnp.where(sub == 7, down[(t + 1) % 6], down[t])
                m = jnp.minimum(jnp.minimum(u, d), h[t])
                new.append(jnp.minimum(jnp.maximum(gc[t], jnp.minimum(v[t], m + COARSE_STEP)), kc[t]))
            v = new
        turned = jnp.concatenate(v + [v[0]] * 10, axis=0).T
        cf[...] = turned

    def rows_of(row0, n):
        for d in range(n):
            for t in range(10):
                at = pl.ds(8 * t, 8)
                zz[d, at, :] = jnp.take_along_axis(cf[at, :], (row0 >> 4) + d, axis=1)

    def groups_of(n):
        for d in range(n):
            for t in range(2):
                y = zz[d, pl.ds(7 + 8 * t, 8), :]
                for j in range(1, 8):
                    y = jnp.where((lane >> 4) == j, zz[d, pl.ds(7 + 8 * j + 8 * t, 8), :], y)
                yy[d, pl.ds(8 * t, 8), :] = y

    def levels(row0, n, K, tiles):
        for k in range(K):
            e = ((row0 & 15) + k) >> 4
            for t in range(tiles):
                at = pl.ds(8 * t, 8)
                x = yy[n - 1, at, :]
                for d in range(n - 2, -1, -1):
                    x = jnp.where(e == d, yy[d, at, :], x)
                xb[k, at, :] = x

    def begin(tt, v, k):
        for t in range(AJ):
            at = pl.ds(8 * t, 8)
            x = xb[k, pl.ds((t + 1) // 2, 8, stride=0), :]
            v[k + 1, at, :] = jnp.minimum(jnp.maximum(tt[0, k, at, :], x), tt[1, k, at, :])

    def wrap(v, K, A):
        for t in range(A):
            at = pl.ds(8 * t, 8)
            v[0, at, :] = pltpu.roll(v[K, at, :], 1, 1)
            v[K + 1, at, :] = pltpu.roll(v[1, at, :], 127, 1)

    def inside_start():
        for grp in (1, 2):
            arrived(3 + grp)
            groups(grp, 1, 7)
        for grp in (1, 2):
            keep(grp, cells(grp, range(8)))
        near = [[cp[a, pl.ds(8 * min(max(t - 1, 0), 3), 8), :] for t in range(6)] for a in range(3)]
        coarse_sweeps(*near)

        def rows_to_lanes(i, carry):
            for u in range(5):
                k = 5 * i + u
                for arr in range(2):
                    turn(ti, arr, k, [pl.ds(64 + k, 8, stride=KI), pl.ds(264 + k, 8, stride=KI)])
            return carry

        lax.fori_loop(0, KI // 5, rows_to_lanes, 0)
        for arr in range(2):
            for k in range(KI):
                ti[arr, k, pl.ds(0, 8), :] = pltpu.roll(ti[arr, k, pl.ds(128, 8), :], 16, 1)
                ti[arr, k, pl.ds(136, 8), :] = pltpu.roll(ti[arr, k, pl.ds(8, 8), :], 112, 1)
        row0 = 184 + KI * strip
        rows_of(row0, 3)
        groups_of(3)
        levels(row0, 3, KI, 2)

        def start(k, carry):
            begin(ti, vi, k)
            return carry

        lax.fori_loop(0, KI, start, 0)
        wrap(vi, KI, AJ)

    def inside_sweeps():
        def two(i, carry):
            sweep(vi, wi, ti.at[0], KI, AJ, True)
            sweep(wi, vi, ti.at[0], KI, AJ, True)
            return carry

        lax.fori_loop(0, 2, two, 0)

    def inside_end():
        inside_sweeps()

        def back(i, carry):
            for u in range(5):
                k = 5 * i + u
                t = vi[k + 1, pl.ds(8, 128), :].T
                for j in range(8):
                    for h in range(2):
                        ov[j, pl.ds(56 + k + KI * 8 * h, 8, stride=KI), :] = t[16 * j + 8 * h : 16 * j + 8 * h + 8, :]
            return carry

        lax.fori_loop(0, KI // 5, back, 0)

        def ends_to_lanes(k, carry):
            for arr in range(2):
                turn(te, arr, k, ends_at(k))
            return carry

        lax.fori_loop(0, KE, ends_to_lanes, 0, unroll=KE)
        for k in range(KS):
            for arr in range(2):
                t = jnp.concatenate([gl[arr, j, at, :] for j in (0, 7) for at in sides_at(k)], axis=0).T
                for u in range(AS):
                    x = t[8 * u + 48 : 8 * u + 56, :] if u < 10 else None
                    if u:
                        y = t[8 * u - 8 : 8 * u, :]
                        x = y if x is None else jnp.where(lane < 64, y, x)
                    ts[arr, k, pl.ds(8 * u, 8), :] = x

    row, col = lax.axis_index("row"), lax.axis_index("col")
    early = (col == 0) | ((row == 0) & (lax.rem(col, 4) == 1))
    earliest = (row == 0) & (col == 0)

    @pl.when(early)
    def _():
        inside_start()

    @pl.when(earliest)
    def _():
        inside_sweeps()

    pl.semaphore_wait(barrier, 8)
    for i in (W_, E_, NW_, NE_, SW_, SE_, N_, S_):
        copies[i].start()

    @pl.when(jnp.logical_not(early))
    def _():
        inside_start()

    @pl.when(jnp.logical_not(earliest))
    def _():
        inside_sweeps()

    inside_end()

    def result(i):
        if i < 8:
            j, src, at = i, ov.at[i, pl.ds(72, 368), :], pl.ds(72, 368)
        elif i < 16:
            j, src, at = i - 8, oe.at[i - 8, pl.ds(8, 72), :], pl.ds(0, 72)
        else:
            j, src, at = i - 16, oe.at[i - 16, pl.ds(96, 72), :], pl.ds(440, 72)
        return pltpu.make_async_copy(src, o_h.at[at, pl.ds(128 * j, 128)], out_sem.at[i])

    for i in range(1, 7):
        result(i).start()
    for i in range(8):
        copies[i].wait()

    for arr in range(2):
        up = [jnp.where(north, F32(HUGE), rr[0, 8 * arr + j]) for j in range(8)]
        down = [pltpu.roll(jnp.where(south, F32(HUGE), rr[1, 8 * arr + j]), 2, 0) for j in range(8)]
        for odd in range(2):
            parts = []
            for j in range(8):
                parts.append(jnp.where((sub & 1) == odd, up[j], down[(j + 7) % 8]))
                parts.append(down[(j + 7) % 8])
            ht[arr, odd, :, :] = jnp.concatenate(parts, axis=0).T
    for arr in range(2):
        for k in range(KE):
            for i in range(16):
                at = pl.ds(8 + 8 * i, 8)
                h = pltpu.roll(ht[arr, k % 2, pl.ds(8 * i, 8), :], (128 - k) % 128, 1)
                x = te[arr, k, at, :]
                if k < 8:
                    x = jnp.where(strip == 0, h, x)
                if k >= 3:
                    x = jnp.where(strip == 15, h, x)
                te[arr, k, at, :] = x
        edge = []
        for side in range(2):
            up, down = (pltpu.roll(dr[side, i, 0], 126, 1) if arr else dr[side, i, 0] for i in range(2))
            up = jnp.where(north, F32(HUGE), up)
            down = jnp.where(south, F32(HUGE), down)
            e = [er[side, arr], pltpu.roll(er[side, 9], 80, 1) if arr else er[side, 9]]
            e[0] = jnp.where(strip == 0, up, e[0])
            e[0] = jnp.where((strip == 15) & (lane >= 63), down, e[0])
            e[1] = jnp.where((strip == 15) & (lane < 48), down, e[1])
            edge.append(e)
        for k in range(KE):
            own = pltpu.roll(te[arr, k, pl.ds(128, 8), :], 16, 1)
            got = pltpu.roll(edge[0][k // 8], (128 - 16 * (k % 8)) % 128, 1)
            te[arr, k, pl.ds(0, 8), :] = jnp.where(lane < 16, got, own)
            own = pltpu.roll(te[arr, k, pl.ds(8, 8), :], 112, 1)
            got = pltpu.roll(edge[1][k // 8], (112 - 16 * (k % 8)) % 128, 1)
            te[arr, k, pl.ds(136, 8), :] = jnp.where(lane >= 112, got, own)
        for k in range(KS):
            west, east = er[0, 2 + 3 * arr + k // 2], er[1, 2 + 3 * arr + k // 2]
            if k % 2:
                west = pltpu.roll(west, 64, 1)
            else:
                east = pltpu.roll(east, 64, 1)
            ts[arr, k, pl.ds(0, 8), :] = jnp.where(lane < 64, west, ts[arr, k, pl.ds(0, 8), :])
            ts[arr, k, pl.ds(80, 8), :] = jnp.where(lane < 64, ts[arr, k, pl.ds(80, 8), :], east)

    rings = []
    for t in range(6):
        if t in (0, 5):
            west, east = (dr[i, t // 5, 1] for i in range(2))
        else:
            west, east = (pltpu.roll(er[i, 8], (b - 24 * t + 24) % 128, 1) for i, b in ((0, 32), (1, 104)))
        rings.append(jnp.where(lane < 64, east, west))
    ext = []
    for a in range(3):
        tiles = []
        for t in range(6):
            ring = pltpu.roll(rings[t], 64 - 8 * a, 1)
            mid = rr[0, 16 + a] if t == 0 else rr[1, 16 + a] if t == 5 else cp[a, pl.ds(8 * t - 8, 8), :]
            x = jnp.where((lane >= 8) & (lane < 72), mid, ring)
            if t == 0:
                x = jnp.where(north, F32(HUGE), x)
            if t == 5:
                x = jnp.where(south, F32(HUGE), x)
            tiles.append(x)
        ext.append(tiles)
    coarse_sweeps(*ext)
    row0 = jnp.where(strip < 8, 120 + KE * strip, 560 + KE * (strip - 8))
    rows_of(row0, 2)
    groups_of(2)
    levels(row0, 2, KE, 2)
    for k in range(KE):
        begin(te, ve, k)
    wrap(ve, KE, AJ)
    row0 = 192 + KS * (lane & 63)
    rows_of(row0, 2)
    for d in range(2):
        yy[d, pl.ds(0, 8), :] = jnp.where(lane < 64, zz[d, pl.ds(7, 8), :], zz[d, pl.ds(67, 8), :])
    levels(row0, 2, KS, 1)
    for k in range(KS):
        for t in range(AS):
            at = pl.ds(8 * t, 8)
            x = jnp.where(lane < 64, xb[k, pl.ds((t + 1) // 2, 8, stride=0), :], xb[k, pl.ds(t // 2, 8, stride=0), :])
            vs[k + 1, at, :] = jnp.minimum(jnp.maximum(ts[0, k, at, :], x), ts[1, k, at, :])
    wrap(vs, KS, AS)

    def two_outer(i, carry):
        sweep(ve, we, te.at[0], KE, AJ, False)
        sweep(vs, ws, ts.at[0], KS, AS, False)
        sweep(we, ve, te.at[0], KE, AJ, False)
        sweep(ws, vs, ts.at[0], KS, AS, False)
        return carry

    lax.fori_loop(0, 4, two_outer, 0)

    for k in range(KE):
        t = ve[k + 1, pl.ds(8, 128), :].T
        for j in range(8):
            for h in range(2):
                oe[j, pl.ds(k + 88 * h, 8, stride=KE), :] = t[16 * j + 8 * h : 16 * j + 8 * h + 8, :]
    for i in range(8, 24):
        result(i).start()
    for k in range(KS):
        v = [vs[k + 1, pl.ds(8 * u, 8), :] for u in range(AS)]
        tiles = [v[u + 1] if u < 7 else jnp.where(lane < 64, v[u + 1], v[u - 6]) if u < 9 else v[u - 6] for u in range(16)]
        t = jnp.concatenate(tiles, axis=0).T
        for m in range(8):
            at = pl.ds(64 + 8 * KS * m + k, 8, stride=KS)
            ov[0, at, :] = jnp.where(lane < 72, t[8 * m : 8 * m + 8, :], ov[0, at, :])
            ov[7, at, :] = jnp.where(lane >= 56, t[64 + 8 * m : 72 + 8 * m, :], ov[7, at, :])
    result(0).start()
    result(7).start()
    for i in range(24):
        result(i).wait()


def tiled(x):
    return x.reshape(64, 8, 8, 128).transpose(0, 2, 1, 3)


def solution(mesh):
    rows, cols = mesh.shape["row"], mesh.shape["col"]

    def shards(elevation, ocean, outlet):
        scratch = [
            pltpu.VMEM((64, 8, 8, 128), F32),
            pltpu.VMEM((64, 8, 8, 128), jnp.int32),
            pltpu.VMEM((64, 8, 8, 128), jnp.int32),
            pltpu.VMEM((2, 8, 528, 128), F32),
            pltpu.VMEM((2, KI, 144, 128), F32),
            pltpu.VMEM((2, KE, 144, 128), F32),
            pltpu.VMEM((2, KS, 88, 128), F32),
            pltpu.VMEM((KI + 2, 144, 128), F32),
            pltpu.VMEM((KI + 2, 144, 128), F32),
            pltpu.VMEM((KE + 2, 144, 128), F32),
            pltpu.VMEM((KE + 2, 144, 128), F32),
            pltpu.VMEM((KS + 2, 88, 128), F32),
            pltpu.VMEM((KS + 2, 88, 128), F32),
            pltpu.VMEM((8, 512, 128), F32),
            pltpu.VMEM((8, 176, 128), F32),
            pltpu.VMEM((3, 8, 32, 128), F32),
            pltpu.VMEM((3, 32, 128), F32),
            pltpu.VMEM((128, 128), F32),
            pltpu.VMEM((4, 80, 128), F32),
            pltpu.VMEM((4, 16, 128), F32),
            pltpu.VMEM((KI, 16, 128), F32),
            pltpu.VMEM((2, 128, 128), F32),
            pltpu.VMEM((2, 19, 8, 128), F32),
            pltpu.VMEM((2, 19, 8, 128), F32),
            pltpu.VMEM((2, 10, 8, 128), F32),
            pltpu.VMEM((2, 10, 8, 128), F32),
            pltpu.VMEM((2, 2, 2, 8, 128), F32),
            pltpu.VMEM((2, 2, 2, 8, 128), F32),
            pltpu.VMEM((2, 2, 128, 128), F32),
            pltpu.SemaphoreType.DMA((6, 3)),
            pltpu.SemaphoreType.DMA((24,)),
            pltpu.SemaphoreType.DMA((8,)),
            pltpu.SemaphoreType.DMA((8,)),
        ]
        return pl.pallas_call(
            lambda *refs: kernel(rows, cols, *refs),
            out_shape=jax.ShapeDtypeStruct((512, 1024), F32),
            in_specs=[pl.BlockSpec(memory_space=pl.ANY)] * 3,
            out_specs=pl.BlockSpec(memory_space=pl.ANY),
            scratch_shapes=scratch,
            name="fill",
            compiler_params=pltpu.CompilerParams(
                collective_id=0, has_side_effects=True, vmem_limit_bytes=50 << 20
            ),
        )(tiled(elevation), tiled(ocean), tiled(outlet))

    return jax.shard_map(
        shards,
        mesh=mesh,
        in_specs=(P("row", "col"), P("row", "col"), P("row", "col")),
        out_specs=P("row", "col"),
        check_vma=False,
    )
```

```python
import jax
import jax.numpy as jnp
from jax import lax
from jax.experimental import pallas as pl
from jax.experimental.pallas import tpu as pltpu
from jax.sharding import PartitionSpec as P

MESH = pl.DeviceIdType.MESH
HUGE = 1e30
FINE_STEP = 2.0 ** (-10)
COARSE_STEP = 2.0 ** (-6)
F32 = jnp.float32

KI, KE, KS = 25, 11, 6
AJ, AS = 18, 11

DIRS = [(-1, 0), (1, 0), (0, -1), (0, 1), (-1, -1), (-1, 1), (1, -1), (1, 1)]
N_, S_, W_, E_, NW_, NE_, SW_, SE_ = range(8)
OPP = [S_, N_, E_, W_, SE_, SW_, NE_, NW_]


def lanes():
    return lax.broadcasted_iota(jnp.int32, (8, 128), 1)


def subs():
    return lax.broadcasted_iota(jnp.int32, (8, 128), 0)


def merge(a, b, w, axis, pos, op):
    size = 8 if axis == 0 else 128
    low = (pos & w) == 0
    p = jnp.where(low, a, b)
    q = jnp.where(low, pltpu.roll(a, size - w, axis), pltpu.roll(b, w, axis))
    return op(p, q)


def tree(xs, ws, axis, pos, op):
    for w in ws:
        half = len(xs) // 2
        xs = [merge(xs[i], xs[i + half], w, axis, pos, op) for i in range(half)]
    return xs[0]


def neighbour(d, rows, cols):
    r = lax.axis_index("row")
    c = lax.axis_index("col")
    return (lax.rem(r + d[0] + rows, rows), lax.rem(c + d[1] + cols, cols))


def sweep(src, dst, g, K, A, loop):
    def row(ref, k):
        return [ref[k, pl.ds(a, 8, stride=A), :] for a in range(A)]

    def across(vm):
        before = pltpu.roll(vm[A - 1], 1, 0)
        after = pltpu.roll(vm[0], 7, 0)
        m = [None] * A
        for a in range(0, A - 1, 2):
            q = jnp.minimum(vm[a], vm[a + 1])
            m[a] = jnp.minimum(vm[a - 1] if a else before, q)
            m[a + 1] = jnp.minimum(q, vm[a + 2] if a + 2 < A else after)
        if A % 2:
            m[A - 1] = jnp.minimum(jnp.minimum(vm[A - 2], vm[A - 1]), after)
        return m

    def put(k, v, m):
        out = []
        for a in range(A):
            x = jnp.maximum(g[k, pl.ds(a, 8, stride=A), :], jnp.minimum(v[a], m[a] + FINE_STEP))
            dst[k + 1, pl.ds(a, 8, stride=A), :] = x
            out.append(x)
        return out

    def pair(k):
        v0, v1, v2, v3 = (row(src, k + i) for i in range(4))
        p = [jnp.minimum(x, y) for x, y in zip(v1, v2)]
        m0 = across([jnp.minimum(x, y) for x, y in zip(v0, p)])
        m1 = across([jnp.minimum(x, y) for x, y in zip(p, v3)])
        return put(k, v1, m0), put(k + 1, v2, m1)

    if K % 2:
        v0, v1, v2 = (row(src, K - 1 + i) for i in range(3))
        last = put(K - 1, v1, across([jnp.minimum(jnp.minimum(x, y), z) for x, y, z in zip(v0, v1, v2)]))
    else:
        last = pair(K - 2)[1]
    for a in range(A):
        dst[0, pl.ds(a, 8, stride=A), :] = pltpu.roll(last[a], 1, 1)
    first, _ = pair(0)
    for a in range(A):
        dst[K + 1, pl.ds(a, 8, stride=A), :] = pltpu.roll(first[a], 127, 1)

    count = (K - 3) // 2 if K % 2 else (K - 4) // 2
    if loop:
        def body(i, c):
            pair(2 + 2 * i)
            return c

        lax.fori_loop(0, count, body, 0)
    else:
        for i in range(count):
            pair(2 + 2 * i)


def kernel(rows, cols, e_h, oc_h, ou_h, o_h, ev, ocv, ouv, gl, ti, te, ts, vi, wi, ve, we, vs, ws, ov, oe, ca, cp, cf, zz,
           yy, xb, cb, rs, rr, es, er, ds, dr, ht, in_sem, out_sem, send, recv):
    lane = lanes()
    sub = subs()
    north = lax.axis_index("row") == 0
    south = lax.axis_index("row") == rows - 1
    to = [neighbour(d, rows, cols) for d in DIRS]

    barrier = pltpu.get_barrier_semaphore()
    for i in (NW_, NE_, SW_, SE_, W_, E_, N_, S_):
        pl.semaphore_signal(barrier, inc=1, device_id=to[i], device_id_type=MESH)

    pieces = [((0, 16), (0, 8)), ((48, 16), (0, 8)), ((16, 32), (0, 1)), ((16, 32), (7, 1)), ((16, 16), (1, 6)), ((32, 16), (1, 6))]

    def loads(p):
        (r, nr), (j, nj) = pieces[p]
        return [pltpu.make_async_copy(h.at[pl.ds(r, nr), pl.ds(j, nj)], v.at[pl.ds(r, nr), pl.ds(j, nj)], in_sem.at[p, i])
                for i, (h, v) in enumerate(((e_h, ev), (oc_h, ocv), (ou_h, ouv)))]

    for p in range(6):
        for c in loads(p):
            c.start()

    def arrived(p):
        for c in loads(p):
            c.wait()

    def group(grp, j):
        gmin, lmin, gmax = [], [], []
        for c in range(8):
            gs, ls = [], []
            for h in range(2):
                r = grp * 16 + 2 * c + h
                oc = ocv[r, j] == 1
                ou = ouv[r, j] == 1
                g = jnp.where(oc, F32(0.0), ev[r, j])
                lk = jnp.where(oc | ou, g, F32(HUGE))
                at = pl.ds(8 * r + 8, 8)
                gl[0, j, at, :] = g
                gl[1, j, at, :] = lk
                gs.append(g)
                ls.append(lk)
            gmin.append(jnp.minimum(*gs))
            lmin.append(jnp.minimum(*ls))
            gmax.append(jnp.maximum(*gs))
        at = pl.ds(grp * 8, 8)
        ca[0, j, at, :] = tree(gmin, (4, 2, 1), 0, sub, jnp.minimum)
        ca[1, j, at, :] = tree(lmin, (4, 2, 1), 0, sub, jnp.minimum)
        ca[2, j, at, :] = tree(gmax, (4, 2, 1), 0, sub, jnp.maximum)

    def groups(grp, lo, hi):
        def body(j, carry):
            group(grp, j)
            return carry

        lax.fori_loop(lo, hi, body, 0, unroll=2)

    arrived(0)
    groups(0, 0, 8)
    arrived(1)
    groups(3, 0, 8)
    for j, p in ((0, 2), (7, 3)):
        arrived(p)
        group(1, j)
        group(2, j)


    def copy(d, src, dst):
        return pltpu.make_async_remote_copy(src_ref=src, dst_ref=dst, send_sem=send.at[d], recv_sem=recv.at[d],
                                            device_id=to[d], device_id_type=MESH)

    copies = [copy(N_, rs.at[0], rr.at[1]), copy(S_, rs.at[1], rr.at[0]),
              copy(W_, es.at[0], er.at[1]), copy(E_, es.at[1], er.at[0]),
              copy(NW_, ds.at[0, 0], dr.at[1, 1]), copy(NE_, ds.at[1, 0], dr.at[0, 1]),
              copy(SW_, ds.at[0, 1], dr.at[1, 0]), copy(SE_, ds.at[1, 1], dr.at[0, 0])]
    for arr in range(2):
        for j in range(8):
            rs[0, 8 * arr + j] = gl[arr, j, pl.ds(8, 8), :]
            rs[1, 8 * arr + j] = gl[arr, j, pl.ds(512, 8), :]

    index = jnp.where((lane >= 8) & (lane < 72), 16 * ((lane - 8) & 7) + 2 * ((lane - 8) >> 3), 0)

    def cells(grp, js):
        out = []
        for a in range(3):
            op = jnp.maximum if a == 2 else jnp.minimum
            x = tree([ca[a, j, pl.ds(8 * grp, 8), :] for j in js], (8, 4, 2), 1, lane, op)
            x = op(x, pltpu.roll(x, 127, 1))
            out.append(jnp.take_along_axis(x, index, axis=1))
        return out

    def keep(grp, x):
        for a in range(3):
            cp[a, pl.ds(8 * grp, 8), :] = x[a]

    packs = []
    for grp in range(4):
        x = cells(grp, range(8) if grp in (0, 3) else (0, 0, 0, 0, 7, 7, 7, 7))
        if grp in (0, 3):
            keep(grp, x)
            for a in range(3):
                rs[grp // 3, 16 + a] = x[a]
        pk = jnp.where(
            ((lane >= 8) & (lane < 16)) | ((lane >= 64) & (lane < 72)), x[0],
            jnp.where(((lane >= 16) & (lane < 24)) | ((lane >= 72) & (lane < 80)),
                      pltpu.roll(x[1], 8, 1), pltpu.roll(x[2], 16, 1)))
        packs.append(pk)
        for side in range(2):
            if grp in (0, 3):
                ds[side, grp // 3, 1] = pk
    strip = lane & 15

    def ends_at(k):
        return [pl.ds(k, 8, stride=KE), pl.ds(440 + k, 8, stride=KE)]

    def sides_at(k):
        return [pl.ds(72 + 8 * KS * m + k, 8, stride=KS) for m in range(8)]

    def outer(arr, at):
        return jnp.where(lane < 64, gl[arr, 0, at, :], gl[arr, 7, at, :])

    def edges_of(arr, ats):
        t = jnp.concatenate([outer(arr, at) for at in ats], axis=0).T
        return t[0:8, :], t[120:128, :]

    rest = []
    corners = []
    for arr in range(2):
        first8 = edges_of(arr, [at for k in range(8) for at in ends_at(k)])
        rest.append(edges_of(arr, [at for k in range(8, 16) for at in ends_at(min(k, KE - 1))]))
        for side in range(2):
            es[side, arr] = first8[side]
        for p in range(3):
            x = edges_of(arr, sides_at(2 * p) + sides_at(2 * p + 1))
            for side in range(2):
                es[side, 2 + 3 * arr + p] = x[side]
        cb[arr, pl.ds(0, 8, stride=16), :] = outer(arr, pl.ds(512, 8))
        cb[arr, pl.ds(15, 8, stride=16), :] = pltpu.roll(outer(arr, pl.ds(8, 8)), 3, 0)
        t = cb[arr].T
        corners.append((t[0:8, :], t[120:128, :]))
    for side in range(2):
        x = packs[0]
        for t in range(4):
            y = pltpu.roll(packs[t], (24 * t + (24 if side == 0 else 96)) % 128, 1)
            x = jnp.where(lane < 32 + 24 * t, x, y)
        es[side, 8] = x
        es[side, 9] = jnp.where(lane < 48, rest[0][side], pltpu.roll(rest[1][side], 48, 1))
        x = jnp.where((strip == 0) | (strip == 15), corners[0][side], pltpu.roll(corners[1][side], 2, 1))
        ds[side, 0, 0] = x
        ds[side, 1, 0] = x

    def turn(dst, arr, k, ats):
        parts = [gl[arr, j, at, :] for j in range(8) for at in ats]
        dst[arr, k, pl.ds(8, 128), :] = jnp.concatenate(parts, axis=0).T

    def coarse_sweeps(gc, kc, v):
        for _ in range(4):
            h = [jnp.minimum(jnp.minimum(pltpu.roll(x, 1, 1), pltpu.roll(x, 127, 1)), x) for x in v]
            up = [pltpu.roll(x, 1, 0) for x in h]
            down = [pltpu.roll(x, 7, 0) for x in h]
            new = []
            for t in range(6):
                u = jnp.where(sub == 0, up[t - 1], up[t])
                d = jnp.where(sub == 7, down[(t + 1) % 6], down[t])
                m = jnp.minimum(jnp.minimum(u, d), h[t])
                new.append(jnp.minimum(jnp.maximum(gc[t], jnp.minimum(v[t], m + COARSE_STEP)), kc[t]))
            v = new
        turned = jnp.concatenate(v + [v[0]] * 10, axis=0).T
        cf[...] = turned

    def rows_of(row0, n):
        for d in range(n):
            for t in range(10):
                at = pl.ds(8 * t, 8)
                zz[d, at, :] = jnp.take_along_axis(cf[at, :], (row0 >> 4) + d, axis=1)

    def groups_of(n):
        for d in range(n):
            for t in range(2):
                y = zz[d, pl.ds(7 + 8 * t, 8), :]
                for j in range(1, 8):
                    y = jnp.where((lane >> 4) == j, zz[d, pl.ds(7 + 8 * j + 8 * t, 8), :], y)
                yy[d, pl.ds(8 * t, 8), :] = y

    def levels(row0, n, K, tiles):
        for k in range(K):
            e = ((row0 & 15) + k) >> 4
            for t in range(tiles):
                at = pl.ds(8 * t, 8)
                x = yy[n - 1, at, :]
                for d in range(n - 2, -1, -1):
                    x = jnp.where(e == d, yy[d, at, :], x)
                xb[k, at, :] = x

    def begin(tt, v, k):
        for t in range(AJ):
            at = pl.ds(8 * t, 8)
            x = xb[k, pl.ds((t + 1) // 2, 8, stride=0), :]
            v[k + 1, at, :] = jnp.minimum(jnp.maximum(tt[0, k, at, :], x), tt[1, k, at, :])

    def wrap(v, K, A):
        for t in range(A):
            at = pl.ds(8 * t, 8)
            v[0, at, :] = pltpu.roll(v[K, at, :], 1, 1)
            v[K + 1, at, :] = pltpu.roll(v[1, at, :], 127, 1)

    def inside_start():
        for grp in (1, 2):
            arrived(3 + grp)
            groups(grp, 1, 7)
        for grp in (1, 2):
            keep(grp, cells(grp, range(8)))
        near = [[cp[a, pl.ds(8 * min(max(t - 1, 0), 3), 8), :] for t in range(6)] for a in range(3)]
        coarse_sweeps(*near)

        def rows_to_lanes(i, carry):
            for u in range(5):
                k = 5 * i + u
                for arr in range(2):
                    turn(ti, arr, k, [pl.ds(64 + k, 8, stride=KI), pl.ds(264 + k, 8, stride=KI)])
            return carry

        lax.fori_loop(0, KI // 5, rows_to_lanes, 0)
        for arr in range(2):
            for k in range(KI):
                ti[arr, k, pl.ds(0, 8), :] = pltpu.roll(ti[arr, k, pl.ds(128, 8), :], 16, 1)
                ti[arr, k, pl.ds(136, 8), :] = pltpu.roll(ti[arr, k, pl.ds(8, 8), :], 112, 1)
        row0 = 184 + KI * strip
        rows_of(row0, 3)
        groups_of(3)
        levels(row0, 3, KI, 2)

        def start(k, carry):
            begin(ti, vi, k)
            return carry

        lax.fori_loop(0, KI, start, 0)
        wrap(vi, KI, AJ)

    def inside_sweeps():
        def two(i, carry):
            sweep(vi, wi, ti.at[0], KI, AJ, True)
            sweep(wi, vi, ti.at[0], KI, AJ, True)
            return carry

        lax.fori_loop(0, 2, two, 0)

    def inside_end():
        inside_sweeps()

        def back(i, carry):
            for u in range(5):
                k = 5 * i + u
                t = vi[k + 1, pl.ds(8, 128), :].T
                for j in range(8):
                    for h in range(2):
                        ov[j, pl.ds(56 + k + KI * 8 * h, 8, stride=KI), :] = t[16 * j + 8 * h : 16 * j + 8 * h + 8, :]
            return carry

        lax.fori_loop(0, KI // 5, back, 0)

        def ends_to_lanes(k, carry):
            for arr in range(2):
                turn(te, arr, k, ends_at(k))
            return carry

        lax.fori_loop(0, KE, ends_to_lanes, 0, unroll=KE)
        for k in range(KS):
            for arr in range(2):
                t = jnp.concatenate([gl[arr, j, at, :] for j in (0, 7) for at in sides_at(k)], axis=0).T
                for u in range(AS):
                    x = t[8 * u + 48 : 8 * u + 56, :] if u < 10 else None
                    if u:
                        y = t[8 * u - 8 : 8 * u, :]
                        x = y if x is None else jnp.where(lane < 64, y, x)
                    ts[arr, k, pl.ds(8 * u, 8), :] = x

    row, col = lax.axis_index("row"), lax.axis_index("col")
    early = (col == 0) | ((row == 0) & (lax.rem(col, 4) == 1))
    earliest = (row == 0) & (col == 0)

    @pl.when(early)
    def _():
        inside_start()

    @pl.when(earliest)
    def _():
        inside_sweeps()

    pl.semaphore_wait(barrier, 8)
    for i in (W_, E_, NW_, NE_, SW_, SE_, N_, S_):
        copies[i].start()

    @pl.when(jnp.logical_not(early))
    def _():
        inside_start()

    @pl.when(jnp.logical_not(earliest))
    def _():
        inside_sweeps()

    inside_end()

    def result(i):
        if i < 8:
            j, src, at = i, ov.at[i, pl.ds(72, 368), :], pl.ds(72, 368)
        elif i < 16:
            j, src, at = i - 8, oe.at[i - 8, pl.ds(8, 72), :], pl.ds(0, 72)
        else:
            j, src, at = i - 16, oe.at[i - 16, pl.ds(96, 72), :], pl.ds(440, 72)
        return pltpu.make_async_copy(src, o_h.at[at, pl.ds(128 * j, 128)], out_sem.at[i])

    for i in range(1, 7):
        result(i).start()
    for i in range(8):
        copies[i].wait()

    rings = []
    for t in range(6):
        if t in (0, 5):
            west, east = (dr[i, t // 5, 1] for i in range(2))
        else:
            west, east = (pltpu.roll(er[i, 8], (b - 24 * t + 24) % 128, 1) for i, b in ((0, 32), (1, 104)))
        rings.append(jnp.where(lane < 64, east, west))
    ext = []
    for a in range(3):
        tiles = []
        for t in range(6):
            ring = pltpu.roll(rings[t], 64 - 8 * a, 1)
            mid = rr[0, 16 + a] if t == 0 else rr[1, 16 + a] if t == 5 else cp[a, pl.ds(8 * t - 8, 8), :]
            x = jnp.where((lane >= 8) & (lane < 72), mid, ring)
            if t == 0:
                x = jnp.where(north, F32(HUGE), x)
            if t == 5:
                x = jnp.where(south, F32(HUGE), x)
            tiles.append(x)
        ext.append(tiles)
    coarse_sweeps(*ext)
    row0 = jnp.where(strip < 8, 120 + KE * strip, 560 + KE * (strip - 8))
    rows_of(row0, 2)
    groups_of(2)
    levels(row0, 2, KE, 2)
    for arr in range(2):
        up = [jnp.where(north, F32(HUGE), rr[0, 8 * arr + j]) for j in range(8)]
        down = [pltpu.roll(jnp.where(south, F32(HUGE), rr[1, 8 * arr + j]), 2, 0) for j in range(8)]
        for odd in range(2):
            parts = []
            for j in range(8):
                parts.append(jnp.where((sub & 1) == odd, up[j], down[(j + 7) % 8]))
                parts.append(down[(j + 7) % 8])
            ht[arr, odd, :, :] = jnp.concatenate(parts, axis=0).T
    for arr in range(2):
        for k in range(KE):
            for i in range(16):
                at = pl.ds(8 + 8 * i, 8)
                h = pltpu.roll(ht[arr, k % 2, pl.ds(8 * i, 8), :], (128 - k) % 128, 1)
                x = te[arr, k, at, :]
                if k < 8:
                    x = jnp.where(strip == 0, h, x)
                if k >= 3:
                    x = jnp.where(strip == 15, h, x)
                te[arr, k, at, :] = x
        edge = []
        for side in range(2):
            up, down = (pltpu.roll(dr[side, i, 0], 126, 1) if arr else dr[side, i, 0] for i in range(2))
            up = jnp.where(north, F32(HUGE), up)
            down = jnp.where(south, F32(HUGE), down)
            e = [er[side, arr], pltpu.roll(er[side, 9], 80, 1) if arr else er[side, 9]]
            e[0] = jnp.where(strip == 0, up, e[0])
            e[0] = jnp.where((strip == 15) & (lane >= 63), down, e[0])
            e[1] = jnp.where((strip == 15) & (lane < 48), down, e[1])
            edge.append(e)
        for k in range(KE):
            own = pltpu.roll(te[arr, k, pl.ds(128, 8), :], 16, 1)
            got = pltpu.roll(edge[0][k // 8], (128 - 16 * (k % 8)) % 128, 1)
            te[arr, k, pl.ds(0, 8), :] = jnp.where(lane < 16, got, own)
            own = pltpu.roll(te[arr, k, pl.ds(8, 8), :], 112, 1)
            got = pltpu.roll(edge[1][k // 8], (112 - 16 * (k % 8)) % 128, 1)
            te[arr, k, pl.ds(136, 8), :] = jnp.where(lane >= 112, got, own)
        for k in range(KS):
            west, east = er[0, 2 + 3 * arr + k // 2], er[1, 2 + 3 * arr + k // 2]
            if k % 2:
                west = pltpu.roll(west, 64, 1)
            else:
                east = pltpu.roll(east, 64, 1)
            ts[arr, k, pl.ds(0, 8), :] = jnp.where(lane < 64, west, ts[arr, k, pl.ds(0, 8), :])
            ts[arr, k, pl.ds(80, 8), :] = jnp.where(lane < 64, ts[arr, k, pl.ds(80, 8), :], east)

    for k in range(KE):
        begin(te, ve, k)
    wrap(ve, KE, AJ)
    row0 = 192 + KS * (lane & 63)
    rows_of(row0, 2)
    for d in range(2):
        yy[d, pl.ds(0, 8), :] = jnp.where(lane < 64, zz[d, pl.ds(7, 8), :], zz[d, pl.ds(67, 8), :])
    levels(row0, 2, KS, 1)
    for k in range(KS):
        for t in range(AS):
            at = pl.ds(8 * t, 8)
            x = jnp.where(lane < 64, xb[k, pl.ds((t + 1) // 2, 8, stride=0), :], xb[k, pl.ds(t // 2, 8, stride=0), :])
            vs[k + 1, at, :] = jnp.minimum(jnp.maximum(ts[0, k, at, :], x), ts[1, k, at, :])
    wrap(vs, KS, AS)

    def two_outer(i, carry):
        sweep(ve, we, te.at[0], KE, AJ, False)
        sweep(vs, ws, ts.at[0], KS, AS, False)
        sweep(we, ve, te.at[0], KE, AJ, False)
        sweep(ws, vs, ts.at[0], KS, AS, False)
        return carry

    lax.fori_loop(0, 4, two_outer, 0)

    for k in range(KE):
        t = ve[k + 1, pl.ds(8, 128), :].T
        for j in range(8):
            for h in range(2):
                oe[j, pl.ds(k + 88 * h, 8, stride=KE), :] = t[16 * j + 8 * h : 16 * j + 8 * h + 8, :]
    for i in range(8, 24):
        result(i).start()
    for k in range(KS):
        v = [vs[k + 1, pl.ds(8 * u, 8), :] for u in range(AS)]
        tiles = [v[u + 1] if u < 7 else jnp.where(lane < 64, v[u + 1], v[u - 6]) if u < 9 else v[u - 6] for u in range(16)]
        t = jnp.concatenate(tiles, axis=0).T
        for m in range(8):
            at = pl.ds(64 + 8 * KS * m + k, 8, stride=KS)
            ov[0, at, :] = jnp.where(lane < 72, t[8 * m : 8 * m + 8, :], ov[0, at, :])
            ov[7, at, :] = jnp.where(lane >= 56, t[64 + 8 * m : 72 + 8 * m, :], ov[7, at, :])
    result(0).start()
    result(7).start()
    for i in range(24):
        result(i).wait()


def tiled(x):
    return x.reshape(64, 8, 8, 128).transpose(0, 2, 1, 3)


def solution(mesh):
    rows, cols = mesh.shape["row"], mesh.shape["col"]

    def shards(elevation, ocean, outlet):
        scratch = [
            pltpu.VMEM((64, 8, 8, 128), F32),
            pltpu.VMEM((64, 8, 8, 128), jnp.int32),
            pltpu.VMEM((64, 8, 8, 128), jnp.int32),
            pltpu.VMEM((2, 8, 528, 128), F32),
            pltpu.VMEM((2, KI, 144, 128), F32),
            pltpu.VMEM((2, KE, 144, 128), F32),
            pltpu.VMEM((2, KS, 88, 128), F32),
            pltpu.VMEM((KI + 2, 144, 128), F32),
            pltpu.VMEM((KI + 2, 144, 128), F32),
            pltpu.VMEM((KE + 2, 144, 128), F32),
            pltpu.VMEM((KE + 2, 144, 128), F32),
            pltpu.VMEM((KS + 2, 88, 128), F32),
            pltpu.VMEM((KS + 2, 88, 128), F32),
            pltpu.VMEM((8, 512, 128), F32),
            pltpu.VMEM((8, 176, 128), F32),
            pltpu.VMEM((3, 8, 32, 128), F32),
            pltpu.VMEM((3, 32, 128), F32),
            pltpu.VMEM((128, 128), F32),
            pltpu.VMEM((4, 80, 128), F32),
            pltpu.VMEM((4, 16, 128), F32),
            pltpu.VMEM((KI, 16, 128), F32),
            pltpu.VMEM((2, 128, 128), F32),
            pltpu.VMEM((2, 19, 8, 128), F32),
            pltpu.VMEM((2, 19, 8, 128), F32),
            pltpu.VMEM((2, 10, 8, 128), F32),
            pltpu.VMEM((2, 10, 8, 128), F32),
            pltpu.VMEM((2, 2, 2, 8, 128), F32),
            pltpu.VMEM((2, 2, 2, 8, 128), F32),
            pltpu.VMEM((2, 2, 128, 128), F32),
            pltpu.SemaphoreType.DMA((6, 3)),
            pltpu.SemaphoreType.DMA((24,)),
            pltpu.SemaphoreType.DMA((8,)),
            pltpu.SemaphoreType.DMA((8,)),
        ]
        return pl.pallas_call(
            lambda *refs: kernel(rows, cols, *refs),
            out_shape=jax.ShapeDtypeStruct((512, 1024), F32),
            in_specs=[pl.BlockSpec(memory_space=pl.ANY)] * 3,
            out_specs=pl.BlockSpec(memory_space=pl.ANY),
            scratch_shapes=scratch,
            name="fill",
            compiler_params=pltpu.CompilerParams(
                collective_id=0, has_side_effects=True, vmem_limit_bytes=50 << 20
            ),
        )(tiled(elevation), tiled(ocean), tiled(outlet))

    return jax.shard_map(
        shards,
        mesh=mesh,
        in_specs=(P("row", "col"), P("row", "col"), P("row", "col")),
        out_specs=P("row", "col"),
        check_vma=False,
    )
```

```python
import jax
import jax.numpy as jnp
from jax import lax
from jax.experimental import pallas as pl
from jax.experimental.pallas import tpu as pltpu
from jax.sharding import PartitionSpec as P

MESH = pl.DeviceIdType.MESH
HUGE = 1e30
FINE_STEP = 2.0 ** (-10)
COARSE_STEP = 2.0 ** (-6)
F32 = jnp.float32

KI, KE, KS = 25, 11, 6
AJ, AS = 18, 11

DIRS = [(-1, 0), (1, 0), (0, -1), (0, 1), (-1, -1), (-1, 1), (1, -1), (1, 1)]
N_, S_, W_, E_, NW_, NE_, SW_, SE_ = range(8)
OPP = [S_, N_, E_, W_, SE_, SW_, NE_, NW_]


def lanes():
    return lax.broadcasted_iota(jnp.int32, (8, 128), 1)


def subs():
    return lax.broadcasted_iota(jnp.int32, (8, 128), 0)


def merge(a, b, w, axis, pos, op):
    size = 8 if axis == 0 else 128
    low = (pos & w) == 0
    p = jnp.where(low, a, b)
    q = jnp.where(low, pltpu.roll(a, size - w, axis), pltpu.roll(b, w, axis))
    return op(p, q)


def tree(xs, ws, axis, pos, op):
    for w in ws:
        half = len(xs) // 2
        xs = [merge(xs[i], xs[i + half], w, axis, pos, op) for i in range(half)]
    return xs[0]


def neighbour(d, rows, cols):
    r = lax.axis_index("row")
    c = lax.axis_index("col")
    return (lax.rem(r + d[0] + rows, rows), lax.rem(c + d[1] + cols, cols))


def sweep(src, dst, g, K, A, loop):
    def row(ref, k):
        return [ref[k, pl.ds(a, 8, stride=A), :] for a in range(A)]

    def across(vm):
        before = pltpu.roll(vm[A - 1], 1, 0)
        after = pltpu.roll(vm[0], 7, 0)
        m = [None] * A
        for a in range(0, A - 1, 2):
            q = jnp.minimum(vm[a], vm[a + 1])
            m[a] = jnp.minimum(vm[a - 1] if a else before, q)
            m[a + 1] = jnp.minimum(q, vm[a + 2] if a + 2 < A else after)
        if A % 2:
            m[A - 1] = jnp.minimum(jnp.minimum(vm[A - 2], vm[A - 1]), after)
        return m

    def put(k, v, m):
        out = []
        for a in range(A):
            x = jnp.maximum(g[k, pl.ds(a, 8, stride=A), :], jnp.minimum(v[a], m[a] + FINE_STEP))
            dst[k + 1, pl.ds(a, 8, stride=A), :] = x
            out.append(x)
        return out

    def pair(k):
        v0, v1, v2, v3 = (row(src, k + i) for i in range(4))
        p = [jnp.minimum(x, y) for x, y in zip(v1, v2)]
        m0 = across([jnp.minimum(x, y) for x, y in zip(v0, p)])
        m1 = across([jnp.minimum(x, y) for x, y in zip(p, v3)])
        return put(k, v1, m0), put(k + 1, v2, m1)

    if K % 2:
        v0, v1, v2 = (row(src, K - 1 + i) for i in range(3))
        last = put(K - 1, v1, across([jnp.minimum(jnp.minimum(x, y), z) for x, y, z in zip(v0, v1, v2)]))
    else:
        last = pair(K - 2)[1]
    for a in range(A):
        dst[0, pl.ds(a, 8, stride=A), :] = pltpu.roll(last[a], 1, 1)
    first, _ = pair(0)
    for a in range(A):
        dst[K + 1, pl.ds(a, 8, stride=A), :] = pltpu.roll(first[a], 127, 1)

    count = (K - 3) // 2 if K % 2 else (K - 4) // 2
    if loop:
        def body(i, c):
            pair(2 + 2 * i)
            return c

        lax.fori_loop(0, count, body, 0)
    else:
        for i in range(count):
            pair(2 + 2 * i)


def kernel(rows, cols, e_h, oc_h, ou_h, o_h, ev, ocv, ouv, gl, ti, te, ts, vi, wi, ve, we, vs, ws, ov, oe, ca, cp, cf, zz,
           yy, xb, cb, rs, rr, es, er, ds, dr, ht, in_sem, out_sem, send, recv):
    lane = lanes()
    sub = subs()
    north = lax.axis_index("row") == 0
    south = lax.axis_index("row") == rows - 1
    to = [neighbour(d, rows, cols) for d in DIRS]

    barrier = pltpu.get_barrier_semaphore()
    for i in (NW_, NE_, SW_, SE_, W_, E_, N_, S_):
        pl.semaphore_signal(barrier, inc=1, device_id=to[i], device_id_type=MESH)

    pieces = [((0, 16), (0, 4)), ((0, 16), (4, 4)), ((48, 16), (0, 4)), ((48, 16), (4, 4)), ((16, 32), (0, 1)), ((16, 32), (7, 1)), ((16, 16), (1, 6)), ((32, 16), (1, 6))]

    def loads(p):
        (r, nr), (j, nj) = pieces[p]
        return [pltpu.make_async_copy(h.at[pl.ds(r, nr), pl.ds(j, nj)], v.at[pl.ds(r, nr), pl.ds(j, nj)], in_sem.at[p, i])
                for i, (h, v) in enumerate(((e_h, ev), (oc_h, ocv), (ou_h, ouv)))]

    for p in range(8):
        for c in loads(p):
            c.start()

    def arrived(p):
        for c in loads(p):
            c.wait()

    def group(grp, j):
        gmin, lmin, gmax = [], [], []
        for c in range(8):
            gs, ls = [], []
            for h in range(2):
                r = grp * 16 + 2 * c + h
                oc = ocv[r, j] == 1
                ou = ouv[r, j] == 1
                g = jnp.where(oc, F32(0.0), ev[r, j])
                lk = jnp.where(oc | ou, g, F32(HUGE))
                at = pl.ds(8 * r + 8, 8)
                gl[0, j, at, :] = g
                gl[1, j, at, :] = lk
                gs.append(g)
                ls.append(lk)
            gmin.append(jnp.minimum(*gs))
            lmin.append(jnp.minimum(*ls))
            gmax.append(jnp.maximum(*gs))
        at = pl.ds(grp * 8, 8)
        ca[0, j, at, :] = tree(gmin, (4, 2, 1), 0, sub, jnp.minimum)
        ca[1, j, at, :] = tree(lmin, (4, 2, 1), 0, sub, jnp.minimum)
        ca[2, j, at, :] = tree(gmax, (4, 2, 1), 0, sub, jnp.maximum)

    def groups(grp, lo, hi):
        def body(j, carry):
            group(grp, j)
            return carry

        lax.fori_loop(lo, hi, body, 0, unroll=2)

    for p in range(4):
        arrived(p)
        groups(3 * (p // 2), 4 * (p % 2), 4 * (p % 2) + 4)
    for j, p in ((0, 4), (7, 5)):
        arrived(p)
        group(1, j)
        group(2, j)


    def copy(d, src, dst):
        return pltpu.make_async_remote_copy(src_ref=src, dst_ref=dst, send_sem=send.at[d], recv_sem=recv.at[d],
                                            device_id=to[d], device_id_type=MESH)

    copies = [copy(N_, rs.at[0], rr.at[1]), copy(S_, rs.at[1], rr.at[0]),
              copy(W_, es.at[0], er.at[1]), copy(E_, es.at[1], er.at[0]),
              copy(NW_, ds.at[0, 0], dr.at[1, 1]), copy(NE_, ds.at[1, 0], dr.at[0, 1]),
              copy(SW_, ds.at[0, 1], dr.at[1, 0]), copy(SE_, ds.at[1, 1], dr.at[0, 0])]
    for arr in range(2):
        for j in range(8):
            rs[0, 8 * arr + j] = gl[arr, j, pl.ds(8, 8), :]
            rs[1, 8 * arr + j] = gl[arr, j, pl.ds(512, 8), :]

    index = jnp.where((lane >= 8) & (lane < 72), 16 * ((lane - 8) & 7) + 2 * ((lane - 8) >> 3), 0)

    def cells(grp, js):
        out = []
        for a in range(3):
            op = jnp.maximum if a == 2 else jnp.minimum
            x = tree([ca[a, j, pl.ds(8 * grp, 8), :] for j in js], (8, 4, 2), 1, lane, op)
            x = op(x, pltpu.roll(x, 127, 1))
            out.append(jnp.take_along_axis(x, index, axis=1))
        return out

    def keep(grp, x):
        for a in range(3):
            cp[a, pl.ds(8 * grp, 8), :] = x[a]

    packs = []
    for grp in range(4):
        x = cells(grp, range(8) if grp in (0, 3) else (0, 0, 0, 0, 7, 7, 7, 7))
        if grp in (0, 3):
            keep(grp, x)
            for a in range(3):
                rs[grp // 3, 16 + a] = x[a]
        pk = jnp.where(
            ((lane >= 8) & (lane < 16)) | ((lane >= 64) & (lane < 72)), x[0],
            jnp.where(((lane >= 16) & (lane < 24)) | ((lane >= 72) & (lane < 80)),
                      pltpu.roll(x[1], 8, 1), pltpu.roll(x[2], 16, 1)))
        packs.append(pk)
        for side in range(2):
            if grp in (0, 3):
                ds[side, grp // 3, 1] = pk
    strip = lane & 15

    def ends_at(k):
        return [pl.ds(k, 8, stride=KE), pl.ds(440 + k, 8, stride=KE)]

    def sides_at(k):
        return [pl.ds(72 + 8 * KS * m + k, 8, stride=KS) for m in range(8)]

    def outer(arr, at):
        return jnp.where(lane < 64, gl[arr, 0, at, :], gl[arr, 7, at, :])

    def edges_of(arr, ats):
        t = jnp.concatenate([outer(arr, at) for at in ats], axis=0).T
        return t[0:8, :], t[120:128, :]

    rest = []
    corners = []
    for arr in range(2):
        first8 = edges_of(arr, [at for k in range(8) for at in ends_at(k)])
        rest.append(edges_of(arr, [at for k in range(8, 16) for at in ends_at(min(k, KE - 1))]))
        for side in range(2):
            es[side, arr] = first8[side]
        for p in range(3):
            x = edges_of(arr, sides_at(2 * p) + sides_at(2 * p + 1))
            for side in range(2):
                es[side, 2 + 3 * arr + p] = x[side]
        cb[arr, pl.ds(0, 8, stride=16), :] = outer(arr, pl.ds(512, 8))
        cb[arr, pl.ds(15, 8, stride=16), :] = pltpu.roll(outer(arr, pl.ds(8, 8)), 3, 0)
        t = cb[arr].T
        corners.append((t[0:8, :], t[120:128, :]))
    for side in range(2):
        x = packs[0]
        for t in range(4):
            y = pltpu.roll(packs[t], (24 * t + (24 if side == 0 else 96)) % 128, 1)
            x = jnp.where(lane < 32 + 24 * t, x, y)
        es[side, 8] = x
        es[side, 9] = jnp.where(lane < 48, rest[0][side], pltpu.roll(rest[1][side], 48, 1))
        x = jnp.where((strip == 0) | (strip == 15), corners[0][side], pltpu.roll(corners[1][side], 2, 1))
        ds[side, 0, 0] = x
        ds[side, 1, 0] = x

    def turn(dst, arr, k, ats):
        parts = [gl[arr, j, at, :] for j in range(8) for at in ats]
        dst[arr, k, pl.ds(8, 128), :] = jnp.concatenate(parts, axis=0).T

    def coarse_sweeps(gc, kc, v):
        for _ in range(4):
            h = [jnp.minimum(jnp.minimum(pltpu.roll(x, 1, 1), pltpu.roll(x, 127, 1)), x) for x in v]
            up = [pltpu.roll(x, 1, 0) for x in h]
            down = [pltpu.roll(x, 7, 0) for x in h]
            new = []
            for t in range(6):
                u = jnp.where(sub == 0, up[t - 1], up[t])
                d = jnp.where(sub == 7, down[(t + 1) % 6], down[t])
                m = jnp.minimum(jnp.minimum(u, d), h[t])
                new.append(jnp.minimum(jnp.maximum(gc[t], jnp.minimum(v[t], m + COARSE_STEP)), kc[t]))
            v = new
        turned = jnp.concatenate(v + [v[0]] * 10, axis=0).T
        cf[...] = turned

    def rows_of(row0, n):
        for d in range(n):
            for t in range(10):
                at = pl.ds(8 * t, 8)
                zz[d, at, :] = jnp.take_along_axis(cf[at, :], (row0 >> 4) + d, axis=1)

    def groups_of(n):
        for d in range(n):
            for t in range(2):
                y = zz[d, pl.ds(7 + 8 * t, 8), :]
                for j in range(1, 8):
                    y = jnp.where((lane >> 4) == j, zz[d, pl.ds(7 + 8 * j + 8 * t, 8), :], y)
                yy[d, pl.ds(8 * t, 8), :] = y

    def levels(row0, n, K, tiles):
        for k in range(K):
            e = ((row0 & 15) + k) >> 4
            for t in range(tiles):
                at = pl.ds(8 * t, 8)
                x = yy[n - 1, at, :]
                for d in range(n - 2, -1, -1):
                    x = jnp.where(e == d, yy[d, at, :], x)
                xb[k, at, :] = x

    def begin(tt, v, k):
        for t in range(AJ):
            at = pl.ds(8 * t, 8)
            x = xb[k, pl.ds((t + 1) // 2, 8, stride=0), :]
            v[k + 1, at, :] = jnp.minimum(jnp.maximum(tt[0, k, at, :], x), tt[1, k, at, :])

    def wrap(v, K, A):
        for t in range(A):
            at = pl.ds(8 * t, 8)
            v[0, at, :] = pltpu.roll(v[K, at, :], 1, 1)
            v[K + 1, at, :] = pltpu.roll(v[1, at, :], 127, 1)

    def inside_start():
        for grp in (1, 2):
            arrived(5 + grp)
            groups(grp, 1, 7)
        for grp in (1, 2):
            keep(grp, cells(grp, range(8)))
        near = [[cp[a, pl.ds(8 * min(max(t - 1, 0), 3), 8), :] for t in range(6)] for a in range(3)]
        coarse_sweeps(*near)

        def rows_to_lanes(i, carry):
            for u in range(5):
                k = 5 * i + u
                for arr in range(2):
                    turn(ti, arr, k, [pl.ds(64 + k, 8, stride=KI), pl.ds(264 + k, 8, stride=KI)])
            return carry

        lax.fori_loop(0, KI // 5, rows_to_lanes, 0)
        for arr in range(2):
            for k in range(KI):
                ti[arr, k, pl.ds(0, 8), :] = pltpu.roll(ti[arr, k, pl.ds(128, 8), :], 16, 1)
                ti[arr, k, pl.ds(136, 8), :] = pltpu.roll(ti[arr, k, pl.ds(8, 8), :], 112, 1)
        row0 = 184 + KI * strip
        rows_of(row0, 3)
        groups_of(3)
        levels(row0, 3, KI, 2)

        def start(k, carry):
            begin(ti, vi, k)
            return carry

        lax.fori_loop(0, KI, start, 0)
        wrap(vi, KI, AJ)

    def inside_sweeps():
        def two(i, carry):
            sweep(vi, wi, ti.at[0], KI, AJ, True)
            sweep(wi, vi, ti.at[0], KI, AJ, True)
            return carry

        lax.fori_loop(0, 2, two, 0)

    def inside_end():
        inside_sweeps()

        def back(i, carry):
            for u in range(5):
                k = 5 * i + u
                t = vi[k + 1, pl.ds(8, 128), :].T
                for j in range(8):
                    for h in range(2):
                        ov[j, pl.ds(56 + k + KI * 8 * h, 8, stride=KI), :] = t[16 * j + 8 * h : 16 * j + 8 * h + 8, :]
            return carry

        lax.fori_loop(0, KI // 5, back, 0)

        def ends_to_lanes(k, carry):
            for arr in range(2):
                turn(te, arr, k, ends_at(k))
            return carry

        lax.fori_loop(0, KE, ends_to_lanes, 0, unroll=KE)
        for k in range(KS):
            for arr in range(2):
                t = jnp.concatenate([gl[arr, j, at, :] for j in (0, 7) for at in sides_at(k)], axis=0).T
                for u in range(AS):
                    x = t[8 * u + 48 : 8 * u + 56, :] if u < 10 else None
                    if u:
                        y = t[8 * u - 8 : 8 * u, :]
                        x = y if x is None else jnp.where(lane < 64, y, x)
                    ts[arr, k, pl.ds(8 * u, 8), :] = x

    row, col = lax.axis_index("row"), lax.axis_index("col")
    early = (col == 0) | ((row == 0) & (lax.rem(col, 4) == 1))
    earliest = (row == 0) & (col == 0)

    @pl.when(early)
    def _():
        inside_start()

    @pl.when(earliest)
    def _():
        inside_sweeps()

    pl.semaphore_wait(barrier, 8)
    for i in (W_, E_, NW_, NE_, SW_, SE_, N_, S_):
        copies[i].start()

    @pl.when(jnp.logical_not(early))
    def _():
        inside_start()

    @pl.when(jnp.logical_not(earliest))
    def _():
        inside_sweeps()

    inside_end()

    def result(i):
        if i < 8:
            j, src, at = i, ov.at[i, pl.ds(72, 368), :], pl.ds(72, 368)
        elif i < 16:
            j, src, at = i - 8, oe.at[i - 8, pl.ds(8, 72), :], pl.ds(0, 72)
        else:
            j, src, at = i - 16, oe.at[i - 16, pl.ds(96, 72), :], pl.ds(440, 72)
        return pltpu.make_async_copy(src, o_h.at[at, pl.ds(128 * j, 128)], out_sem.at[i])

    for i in range(1, 7):
        result(i).start()
    for i in range(8):
        copies[i].wait()

    rings = []
    for t in range(6):
        if t in (0, 5):
            west, east = (dr[i, t // 5, 1] for i in range(2))
        else:
            west, east = (pltpu.roll(er[i, 8], (b - 24 * t + 24) % 128, 1) for i, b in ((0, 32), (1, 104)))
        rings.append(jnp.where(lane < 64, east, west))
    ext = []
    for a in range(3):
        tiles = []
        for t in range(6):
            ring = pltpu.roll(rings[t], 64 - 8 * a, 1)
            mid = rr[0, 16 + a] if t == 0 else rr[1, 16 + a] if t == 5 else cp[a, pl.ds(8 * t - 8, 8), :]
            x = jnp.where((lane >= 8) & (lane < 72), mid, ring)
            if t == 0:
                x = jnp.where(north, F32(HUGE), x)
            if t == 5:
                x = jnp.where(south, F32(HUGE), x)
            tiles.append(x)
        ext.append(tiles)
    coarse_sweeps(*ext)
    row0 = jnp.where(strip < 8, 120 + KE * strip, 560 + KE * (strip - 8))
    rows_of(row0, 2)
    groups_of(2)
    levels(row0, 2, KE, 2)
    for arr in range(2):
        up = [jnp.where(north, F32(HUGE), rr[0, 8 * arr + j]) for j in range(8)]
        down = [pltpu.roll(jnp.where(south, F32(HUGE), rr[1, 8 * arr + j]), 2, 0) for j in range(8)]
        for odd in range(2):
            parts = []
            for j in range(8):
                parts.append(jnp.where((sub & 1) == odd, up[j], down[(j + 7) % 8]))
                parts.append(down[(j + 7) % 8])
            ht[arr, odd, :, :] = jnp.concatenate(parts, axis=0).T
    for arr in range(2):
        for k in range(KE):
            for i in range(16):
                at = pl.ds(8 + 8 * i, 8)
                h = pltpu.roll(ht[arr, k % 2, pl.ds(8 * i, 8), :], (128 - k) % 128, 1)
                x = te[arr, k, at, :]
                if k < 8:
                    x = jnp.where(strip == 0, h, x)
                if k >= 3:
                    x = jnp.where(strip == 15, h, x)
                te[arr, k, at, :] = x
        edge = []
        for side in range(2):
            up, down = (pltpu.roll(dr[side, i, 0], 126, 1) if arr else dr[side, i, 0] for i in range(2))
            up = jnp.where(north, F32(HUGE), up)
            down = jnp.where(south, F32(HUGE), down)
            e = [er[side, arr], pltpu.roll(er[side, 9], 80, 1) if arr else er[side, 9]]
            e[0] = jnp.where(strip == 0, up, e[0])
            e[0] = jnp.where((strip == 15) & (lane >= 63), down, e[0])
            e[1] = jnp.where((strip == 15) & (lane < 48), down, e[1])
            edge.append(e)
        for k in range(KE):
            own = pltpu.roll(te[arr, k, pl.ds(128, 8), :], 16, 1)
            got = pltpu.roll(edge[0][k // 8], (128 - 16 * (k % 8)) % 128, 1)
            te[arr, k, pl.ds(0, 8), :] = jnp.where(lane < 16, got, own)
            own = pltpu.roll(te[arr, k, pl.ds(8, 8), :], 112, 1)
            got = pltpu.roll(edge[1][k // 8], (112 - 16 * (k % 8)) % 128, 1)
            te[arr, k, pl.ds(136, 8), :] = jnp.where(lane >= 112, got, own)
        for k in range(KS):
            west, east = er[0, 2 + 3 * arr + k // 2], er[1, 2 + 3 * arr + k // 2]
            if k % 2:
                west = pltpu.roll(west, 64, 1)
            else:
                east = pltpu.roll(east, 64, 1)
            ts[arr, k, pl.ds(0, 8), :] = jnp.where(lane < 64, west, ts[arr, k, pl.ds(0, 8), :])
            ts[arr, k, pl.ds(80, 8), :] = jnp.where(lane < 64, ts[arr, k, pl.ds(80, 8), :], east)

    for k in range(KE):
        begin(te, ve, k)
    wrap(ve, KE, AJ)
    row0 = 192 + KS * (lane & 63)
    rows_of(row0, 2)
    for d in range(2):
        yy[d, pl.ds(0, 8), :] = jnp.where(lane < 64, zz[d, pl.ds(7, 8), :], zz[d, pl.ds(67, 8), :])
    levels(row0, 2, KS, 1)
    for k in range(KS):
        for t in range(AS):
            at = pl.ds(8 * t, 8)
            x = jnp.where(lane < 64, xb[k, pl.ds((t + 1) // 2, 8, stride=0), :], xb[k, pl.ds(t // 2, 8, stride=0), :])
            vs[k + 1, at, :] = jnp.minimum(jnp.maximum(ts[0, k, at, :], x), ts[1, k, at, :])
    wrap(vs, KS, AS)

    def two_outer(i, carry):
        sweep(ve, we, te.at[0], KE, AJ, False)
        sweep(vs, ws, ts.at[0], KS, AS, False)
        sweep(we, ve, te.at[0], KE, AJ, False)
        sweep(ws, vs, ts.at[0], KS, AS, False)
        return carry

    lax.fori_loop(0, 4, two_outer, 0)

    for k in range(KE):
        t = ve[k + 1, pl.ds(8, 128), :].T
        for j in range(8):
            for h in range(2):
                oe[j, pl.ds(k + 88 * h, 8, stride=KE), :] = t[16 * j + 8 * h : 16 * j + 8 * h + 8, :]
    for i in range(8, 24):
        result(i).start()
    for k in range(KS):
        v = [vs[k + 1, pl.ds(8 * u, 8), :] for u in range(AS)]
        tiles = [v[u + 1] if u < 7 else jnp.where(lane < 64, v[u + 1], v[u - 6]) if u < 9 else v[u - 6] for u in range(16)]
        t = jnp.concatenate(tiles, axis=0).T
        for m in range(8):
            at = pl.ds(64 + 8 * KS * m + k, 8, stride=KS)
            ov[0, at, :] = jnp.where(lane < 72, t[8 * m : 8 * m + 8, :], ov[0, at, :])
            ov[7, at, :] = jnp.where(lane >= 56, t[64 + 8 * m : 72 + 8 * m, :], ov[7, at, :])
    result(0).start()
    result(7).start()
    for i in range(24):
        result(i).wait()


def tiled(x):
    return x.reshape(64, 8, 8, 128).transpose(0, 2, 1, 3)


def solution(mesh):
    rows, cols = mesh.shape["row"], mesh.shape["col"]

    def shards(elevation, ocean, outlet):
        scratch = [
            pltpu.VMEM((64, 8, 8, 128), F32),
            pltpu.VMEM((64, 8, 8, 128), jnp.int32),
            pltpu.VMEM((64, 8, 8, 128), jnp.int32),
            pltpu.VMEM((2, 8, 528, 128), F32),
            pltpu.VMEM((2, KI, 144, 128), F32),
            pltpu.VMEM((2, KE, 144, 128), F32),
            pltpu.VMEM((2, KS, 88, 128), F32),
            pltpu.VMEM((KI + 2, 144, 128), F32),
            pltpu.VMEM((KI + 2, 144, 128), F32),
            pltpu.VMEM((KE + 2, 144, 128), F32),
            pltpu.VMEM((KE + 2, 144, 128), F32),
            pltpu.VMEM((KS + 2, 88, 128), F32),
            pltpu.VMEM((KS + 2, 88, 128), F32),
            pltpu.VMEM((8, 512, 128), F32),
            pltpu.VMEM((8, 176, 128), F32),
            pltpu.VMEM((3, 8, 32, 128), F32),
            pltpu.VMEM((3, 32, 128), F32),
            pltpu.VMEM((128, 128), F32),
            pltpu.VMEM((4, 80, 128), F32),
            pltpu.VMEM((4, 16, 128), F32),
            pltpu.VMEM((KI, 16, 128), F32),
            pltpu.VMEM((2, 128, 128), F32),
            pltpu.VMEM((2, 19, 8, 128), F32),
            pltpu.VMEM((2, 19, 8, 128), F32),
            pltpu.VMEM((2, 10, 8, 128), F32),
            pltpu.VMEM((2, 10, 8, 128), F32),
            pltpu.VMEM((2, 2, 2, 8, 128), F32),
            pltpu.VMEM((2, 2, 2, 8, 128), F32),
            pltpu.VMEM((2, 2, 128, 128), F32),
            pltpu.SemaphoreType.DMA((8, 3)),
            pltpu.SemaphoreType.DMA((24,)),
            pltpu.SemaphoreType.DMA((8,)),
            pltpu.SemaphoreType.DMA((8,)),
        ]
        return pl.pallas_call(
            lambda *refs: kernel(rows, cols, *refs),
            out_shape=jax.ShapeDtypeStruct((512, 1024), F32),
            in_specs=[pl.BlockSpec(memory_space=pl.ANY)] * 3,
            out_specs=pl.BlockSpec(memory_space=pl.ANY),
            scratch_shapes=scratch,
            name="fill",
            compiler_params=pltpu.CompilerParams(
                collective_id=0, has_side_effects=True, vmem_limit_bytes=50 << 20
            ),
        )(tiled(elevation), tiled(ocean), tiled(outlet))

    return jax.shard_map(
        shards,
        mesh=mesh,
        in_specs=(P("row", "col"), P("row", "col"), P("row", "col")),
        out_specs=P("row", "col"),
        check_vma=False,
    )
```
